256 devices in a mesh: occ: 64 (over z, y, x_lo), vir: 4 (over x_hi, core).
Axes of the slice: x: 4 (x_hi: 2, x_lo: 2; x = x_hi * 2 + x_lo), y: 4, z: 8, core: 2. Of those that a mesh axis runs over, the one named last changes fastest.
Arguments:
- factors: bfloat16 [2, 3072, 6144], P(None, 'occ', 'vir'), may hold values from -0.41992188 to 0.41992188
- occ_energy: float32 [2], replicated, may hold values from -1.2 to -0.4
- vir_energy: float32 [3072], replicated, may hold values from 0.4 to 2.5
- block_lengths: int32 [4, 64], replicated, may hold values from 1 to 64, 1536 in all within a row
- block_owner: int32 [4, 64], replicated, may hold values from 0 to 63, each once within a row
Outputs:
- gamma_owned: bfloat16 [16384, 2, 3072], P(('occ', 'vir'))
The draws below stay inside these ranges and needn't reach their ends.
Inputs may be any that keep to these rules, and one draw needn't show every extreme that they name: `block_lengths`: each row sums to 1536, and every row's largest entry is exactly 64. `block_owner`: each row names every owner index once.
All inputs are finite; a program needn't handle non-finite values.
Results may differ from the reference program's by a relative error of at most 0.0037.
Values may be sent and summed in bfloat16 or wider, within the bound.
A program may use at most 64 MiB of HBM per device.

```python
import math
import jax
import jax.numpy as jnp
import numpy as np

V = 3072
P_SIZE = 6144
OCC = 2
PQ = 1536
QUARTERS = 4
BLOCKS = 64
CAP = 64


def block_levels(rng, extent, cuts, smallest, top_value):
    factor_of = 1.0
    for axis_at, blocks in cuts:
        heights = jax.random.uniform(jax.random.fold_in(jax.random.fold_in(rng, 6), axis_at), (blocks,), jnp.float32, smallest / len(cuts), top_value / len(cuts))
        factor_of = factor_of * jnp.repeat(jnp.exp(heights), extent[axis_at] // blocks).reshape((-1,) + (1,) * (len(extent) - 1 - axis_at))
    return factor_of


def length_profile(number_of, total, reach, skew):
    loads = [(1 << 20) // math.isqrt(standing ** skew) + 1 for standing in range(2, number_of + 1)]
    surplus, given = total - reach - (number_of - 1), [1] * (number_of - 1)
    while surplus > 0:
        candidates = [i for i in range(number_of - 1) if given[i] < reach]
        pool, budget = sum([loads[i] for i in candidates]), surplus
        for i in candidates:
            more = min(reach - given[i], max(1, budget * loads[i] // pool), surplus)
            given[i] = given[i] + more
            surplus = surplus - more
    return np.array([reach] + given)


def uneven(stream_key, amount, total, limit, skew):
    if amount == 2:
        one = jax.random.randint(stream_key, (), max(1, total - limit), min(limit, total - 1) + 1)
        return jnp.stack([one, total - one])
    tallies = jnp.asarray(length_profile(amount, total, limit, skew), jnp.int32)
    pairs = (amount - 1) // 2
    donor, taker = tallies[1:1 + 2 * pairs:2], tallies[2:2 + 2 * pairs:2]
    room = jnp.minimum(donor - 1, limit - taker)
    moved = jax.random.randint(jax.random.fold_in(stream_key, 1), (pairs,), 0, 1 << 20) % (room + 1)
    tallies = tallies.at[1:1 + 2 * pairs:2].set(donor - moved).at[2:2 + 2 * pairs:2].set(taker + moved)
    return tallies[jax.random.permutation(jax.random.fold_in(stream_key, 2), amount)]


def normal_values(stream_key, dims, spread, bound, pieces=(), kind=jnp.bfloat16):
    array = spread * jax.random.normal(stream_key, dims, jnp.float32)
    if pieces:
        array = array * block_levels(stream_key, dims, pieces, -0.22, 0.18)
    return jnp.clip(array, -bound, bound).astype(kind)


def setup_inputs(seed: int = 0) -> dict:
    seeds = jax.random.split(jax.random.key(seed), 6)
    factors = normal_values(seeds[0], (OCC, V, P_SIZE), 0.07, 0.41992188, ((1, 64), (2, 4)))
    occ_energy = jnp.clip(jax.random.uniform(seeds[1], (OCC,), jnp.float32, -1.2, -0.4), -1.2, -0.4)
    vir_energy = jnp.clip(jax.random.uniform(seeds[2], (V,), jnp.float32, 0.4, 2.5), 0.4, 2.5)
    block_lengths = jax.vmap(lambda own: uneven(own, BLOCKS, PQ, CAP, 2))(jax.random.split(seeds[3], QUARTERS)).reshape((QUARTERS, BLOCKS)).astype(jnp.int32)
    block_owner = jax.vmap(lambda own: jax.random.permutation(own, BLOCKS))(jax.random.split(seeds[4], QUARTERS)).reshape((QUARTERS, BLOCKS)).astype(jnp.int32)
    return dict(factors=factors, occ_energy=occ_energy, vir_energy=vir_energy, block_lengths=block_lengths, block_owner=block_owner)


def reference(factors, occ_energy, vir_energy, block_lengths, block_owner):
    wide = factors.astype(jnp.float32)
    pair = jnp.einsum("iap,jbp->ijab", wide, wide)
    occupied_sum = occ_energy[:, None] + occ_energy[None, :]
    denominator = occupied_sum[:, :, None, None] - vir_energy[None, None, :, None] - vir_energy[None, None, None, :]
    amplitude = ((2.0 * pair - jnp.transpose(pair, (1, 0, 2, 3))) / denominator).astype(jnp.bfloat16)
    gamma = jnp.einsum("ijab,jbp->iap", amplitude.astype(jnp.float32), wide).astype(jnp.bfloat16)
    quarters = block_lengths.shape[0]
    blocks = block_lengths.shape[1]
    quarter_width = P_SIZE // quarters
    starts = (jnp.cumsum(block_lengths, axis=1) - block_lengths).astype(jnp.int32)
    owner_match = block_owner[:, None, :] == jnp.arange(blocks, dtype=jnp.int32)[None, :, None]
    dest_start = jnp.sum(jnp.where(owner_match, starts[:, None, :], 0), axis=2).astype(jnp.int32)
    dest_length = jnp.sum(jnp.where(owner_match, block_lengths[:, None, :], 0), axis=2).astype(jnp.int32)
    slot_index = jnp.arange(CAP, dtype=jnp.int32)
    offsets = jnp.arange(quarters, dtype=jnp.int32)[:, None, None] * quarter_width
    columns = offsets + jnp.minimum(dest_start[:, :, None] + slot_index[None, None, :], quarter_width - 1)
    live_slot = slot_index[None, None, :] < dest_length[:, :, None]
    columns = jnp.transpose(columns, (1, 0, 2)).reshape(-1).astype(jnp.int32)
    live_slot = jnp.transpose(live_slot, (1, 0, 2)).reshape(-1)
    picked = jnp.take(jnp.transpose(gamma, (2, 0, 1)), columns, axis=0)
    return jnp.where(live_slot[:, None, None], picked, jnp.zeros((), gamma.dtype))
```

```python
import jax
import jax.numpy as jnp
from jax import lax
from jax.sharding import Mesh, PartitionSpec as P

ROW = ("y", "xl")
VIR = ("xh", "core")


def per_device(factors, occ_energy, vir_energy, block_lengths, block_owner):
    zi = lax.axis_index("z")
    yx = lax.axis_index(ROW)
    nz = lax.axis_size("z")
    nyx = lax.axis_size(ROW)
    cycle_size = nz * nyx
    quarter_index = lax.axis_index(VIR)
    occupied, tile_rows, width = factors.shape
    group = tile_rows * nyx
    row_block = lax.all_gather(factors, ROW, axis=1, tiled=True)
    col_block = lax.all_gather(factors, "z", axis=1, tiled=True)
    pair = jnp.einsum("iap,jbp->ijab", row_block, col_block, preferred_element_type=jnp.float32)
    pair = lax.psum(pair.reshape(-1), VIR).reshape(pair.shape)
    occupied_sum = occ_energy[:, None] + occ_energy[None, :]
    row_energy = lax.dynamic_slice_in_dim(vir_energy, zi * group, group)
    col_energy = lax.dynamic_index_in_dim(
        vir_energy.reshape(nz, nyx, tile_rows), yx, 1, keepdims=False
    ).reshape(-1)
    denominator = (
        occupied_sum[:, :, None, None] - row_energy[None, None, :, None] - col_energy[None, None, None, :]
    )
    amplitude = ((2.0 * pair - jnp.transpose(pair, (1, 0, 2, 3))) / denominator).astype(jnp.bfloat16)
    partial = jnp.einsum("ijab,jbp->iap", amplitude, col_block, preferred_element_type=jnp.float32)
    gamma = lax.psum_scatter(partial, ROW, scatter_dimension=1, tiled=True).astype(jnp.bfloat16)
    capacity = 8 * width // (3 * cycle_size)
    lengths_row = lax.dynamic_index_in_dim(block_lengths, quarter_index, 0, keepdims=False)
    owners_row = lax.dynamic_index_in_dim(block_owner, quarter_index, 0, keepdims=False)
    starts_row = jnp.cumsum(lengths_row) - lengths_row
    owner_match = owners_row[None, :] == jnp.arange(cycle_size, dtype=jnp.int32)[:, None]
    dest_start = jnp.sum(jnp.where(owner_match, starts_row[None, :], 0), axis=1)
    dest_length = jnp.sum(jnp.where(owner_match, lengths_row[None, :], 0), axis=1)
    slot_index = jnp.arange(capacity, dtype=jnp.int32)
    columns = jnp.where(
        slot_index[None, :] < dest_length[:, None], dest_start[:, None] + slot_index[None, :], -1
    ).reshape(-1)
    chosen = (columns[:, None] == jnp.arange(width, dtype=jnp.int32)[None, :]).astype(jnp.bfloat16)
    picked = jnp.einsum("sp,iap->sia", chosen, gamma, preferred_element_type=jnp.float32)
    picked = picked.astype(jnp.bfloat16)
    outgoing = picked.reshape(cycle_size, capacity * occupied * tile_rows)
    incoming = lax.all_to_all(outgoing, ("z",) + ROW, split_axis=0, concat_axis=0, tiled=True)
    incoming = incoming.reshape(cycle_size, capacity, occupied, tile_rows)
    return jnp.transpose(incoming, (1, 2, 0, 3)).reshape(capacity, occupied, cycle_size * tile_rows)


def solution(mesh):
    fine = Mesh(mesh.devices.reshape(8, 4, 2, 2, 2), ("z", "y", "xl", "xh", "core"))
    placed = (P(None, ("z", "y", "xl"), VIR), P(), P(), P(), P())
    return jax.shard_map(
        per_device,
        mesh=fine,
        in_specs=placed,
        out_specs=P(("z", "y", "xl", "xh", "core"), None, None),
        check_vma=False,
    )
```

```python
import jax
import jax.numpy as jnp
from jax import lax
from jax.experimental import pallas as pl
from jax.experimental.pallas import tpu as pltpu
from jax.sharding import Mesh, PartitionSpec as P

ROW = ("y", "xl")
VIR = ("xh", "core")
F32 = jnp.float32
BF16 = jnp.bfloat16


def ring(axis, shift):
    n = lax.axis_size(axis)
    return lax.rem(lax.axis_index(axis) + shift + n, n)


def flip(axis):
    return 1 - lax.axis_index(axis)


def gamma_kernel(
    f_ref, occ_ref, row_e_ref, col_e_ref, out_ref,
    rbuf, cbuf, m_send, m_own, m_recv, h_send, h_recv, abuf, part,
    a_send, a_recv, b_send, b_recv, x_out, x_recv,
    zs, zr, ys, yr, xs, xr, ms, mr, hs, hr, as_, ar, pas, par, pbs, pbr, pxs, pxr,
):
    z, y, xl, xh, core = (lax.axis_index(n) for n in ("z", "y", "xl", "xh", "core"))
    rows = f_ref.shape[1]
    width = f_ref.shape[2]

    barrier = pltpu.get_barrier_semaphore()
    peers = [
        {"z": ring("z", 1)}, {"z": ring("z", -1)}, {"y": ring("y", 1)}, {"y": ring("y", -1)},
        {"xl": flip("xl")}, {"xh": flip("xh")}, {"core": flip("core")},
    ]
    for peer in peers:
        pl.semaphore_signal(barrier, inc=1, device_id=peer, device_id_type=pl.DeviceIdType.MESH)
    pl.semaphore_wait(barrier, len(peers))

    started = []

    def send(src, dst, ssem, rsem, peer):
        copy = pltpu.make_async_remote_copy(
            src_ref=src, dst_ref=dst, send_sem=ssem, recv_sem=rsem,
            device_id=peer, device_id_type=pl.DeviceIdType.MESH,
        )
        copy.start()
        started.append(copy)
        return copy

    def arrive(dst, rsem):
        pltpu.make_async_remote_copy(
            src_ref=dst, dst_ref=dst, send_sem=rsem, recv_sem=rsem,
            device_id=peers[0], device_id_type=pl.DeviceIdType.MESH,
        ).wait_recv()

    def yx(dy, other):
        return ring("y", dy) * 2 + (flip("xl") if other else xl)

    z_to = ({"z": ring("z", 1)}, {"z": ring("z", -1)})
    y_to = ({"y": ring("y", 1)}, {"y": ring("y", -1)})
    x_to = {"xl": flip("xl")}

    def z_send(d, step, i):
        origin = ring("z", (1 - step) if d == 0 else (step - 1))
        src = f_ref.at[i] if step == 1 else cbuf.at[i, origin]
        send(src, cbuf.at[i, origin], zs.at[d, step - 1, i], zr.at[d, step - 1, i], z_to[d])

    def z_arrive(d, step, i):
        origin = ring("z", -step if d == 0 else step)
        arrive(cbuf.at[i, origin], zr.at[d, step - 1, i])

    def y_send(d, k, i, dy, other):
        src = f_ref.at[i] if (dy == 0 and not other) else rbuf.at[i, yx(dy, other)]
        send(src, rbuf.at[i, yx(dy, other)], ys.at[d, k], yr.at[d, k], y_to[d])

    def y_arrive(d, k, i, dy, other):
        arrive(rbuf.at[i, yx(dy, other)], yr.at[d, k])

    def x_send(k, i, dy):
        src = f_ref.at[i] if dy == 0 else rbuf.at[i, yx(dy, False)]
        send(src, rbuf.at[i, yx(dy, False)], xs.at[k], xr.at[k], x_to)

    def x_arrive(k, i, dy):
        arrive(rbuf.at[i, yx(dy, True)], xr.at[k])

    for i in (0, 1):
        for d in (0, 1):
            z_send(d, 1, i)
            y_send(d, i, i, 0, False)
        x_send(i, i, 0)
    for i in (0, 1):
        cbuf[i, z] = f_ref[i]
        rbuf[i, yx(0, False)] = f_ref[i]
    for d in (0, 1):
        z_arrive(d, 1, 0)
        z_send(d, 2, 0)
    y_arrive(0, 0, 0, -1, False)
    x_send(2, 0, -1)
    y_send(0, 2, 0, -1, False)
    y_arrive(1, 0, 0, 1, False)
    for d in (0, 1):
        z_arrive(d, 1, 1)
        z_send(d, 2, 1)
    y_arrive(1, 1, 1, 1, False)
    x_send(3, 1, 1)
    y_send(1, 2, 1, 1, False)
    x_send(4, 0, 1)
    y_arrive(0, 1, 1, -1, False)
    x_send(5, 1, -1)
    for d in (0, 1):
        z_arrive(d, 2, 0)
        z_send(d, 3, 0)
    x_arrive(0, 0, 0)
    x_arrive(1, 1, 0)
    x_arrive(2, 0, -1)
    y_send(0, 3, 0, -1, True)
    for d in (0, 1):
        z_arrive(d, 2, 1)
        z_send(d, 3, 1)
    x_arrive(3, 1, 1)
    y_send(1, 3, 1, 1, True)
    z_arrive(0, 3, 0)
    z_send(0, 4, 0)
    z_arrive(1, 3, 1)
    z_send(1, 4, 1)
    z_arrive(1, 3, 0)
    z_arrive(0, 3, 1)
    y_arrive(0, 2, 0, -2, False)
    y_arrive(1, 2, 1, 2, False)
    x_arrive(4, 0, 1)
    x_arrive(5, 1, -1)
    y_arrive(0, 3, 0, -2, True)
    y_arrive(1, 3, 1, 2, True)
    z_arrive(0, 4, 0)
    z_arrive(1, 4, 1)

    half = 4 * rows
    side = 8 * rows
    columns = cbuf[...].reshape(2 * side, width)

    def pair_rows(i, h):
        lhs = rbuf[i, pl.ds(h * 4, 4)].reshape(half, width)
        return lax.dot_general(lhs, columns, (((1,), (1,)), ((), ())), preferred_element_type=F32)

    core_to = {"core": flip("core")}
    for i in (0, 1):
        m_send[i] = pair_rows(i, 1 - core)
        send(m_send.at[i], m_recv.at[i], ms.at[i], mr.at[i], core_to)
    for i in (0, 1):
        m_own[i] = pair_rows(i, core)
    xh_to = {"xh": flip("xh")}
    for i in (0, 1):
        arrive(m_recv.at[i], mr.at[i])
        total = m_own[i] + m_recv[i]
        m_own[i] = total
        h_send[i] = total.astype(BF16)
        send(h_send.at[i], h_recv.at[i], hs.at[i], hr.at[i], xh_to)
    for i in (0, 1):
        arrive(h_recv.at[i], hr.at[i])
        m_own[i] = m_own[i] + h_recv[i].astype(F32)
    row_e = row_e_ref[pl.ds(pl.multiple_of(core * half, 16), half), :]
    col_e = col_e_ref[...]
    mine = pl.ds(pl.multiple_of(core * half, 16), half)
    for i in (0, 1):
        for j in (0, 1):
            denominator = (occ_ref[i] + occ_ref[j]) - row_e - col_e
            direct = m_own[i, :, pl.ds(j * side, side)]
            swapped = m_own[j, :, pl.ds(i * side, side)]
            abuf[i, mine, pl.ds(j * side, side)] = ((2.0 * direct - swapped) / denominator).astype(BF16)
        send(abuf.at[i, mine], abuf.at[i, mine], as_.at[i], ar.at[i], core_to)
    theirs = pl.ds(pl.multiple_of((1 - core) * half, 16), half)
    for i in (0, 1):
        arrive(abuf.at[i, theirs], ar.at[i])

    pair_rows2 = 2 * rows

    def partial(slot, dy):
        at = pl.ds(pl.multiple_of(ring("y", dy) * pair_rows2, 16), pair_rows2)
        lhs = abuf[:, at, :].reshape(2 * pair_rows2, 2 * side)
        res = jnp.dot(lhs, cbuf[...].reshape(2 * side, width), preferred_element_type=F32)
        part[slot] = res.reshape(2, pair_rows2, width)

    partial(0, 2)
    for d in (0, 1):
        a_send[d] = part[0, d].astype(BF16)
        send(a_send.at[d], a_recv.at[d], pas.at[d], par.at[d], y_to[d])
    for d in (0, 1):
        partial(1 + d, 1 if d == 0 else -1)
        i = 1 - d
        b_send[d, i] = part[1 + d, i].astype(BF16)
        send(b_send.at[d, i], b_recv.at[d, i], pbs.at[d, i], pbr.at[d, i], y_to[d])
    for d in (0, 1):
        arrive(a_recv.at[d], par.at[d])
        b_send[d, d] = (part[1 + d, d] + a_recv[d].astype(F32)).astype(BF16)
        send(b_send.at[d, d], b_recv.at[d, d], pbs.at[d, d], pbr.at[d, d], y_to[d])
    partial(0, 0)
    own_rows = pl.ds(pl.multiple_of(xl * rows, 16), rows)
    far_rows = pl.ds(pl.multiple_of((1 - xl) * rows, 16), rows)
    for i in (0, 1):
        for d in (0, 1):
            arrive(b_recv.at[d, i], pbr.at[d, i])
        far = part[0, i, far_rows] + b_recv[0, i, far_rows].astype(F32) + b_recv[1, i, far_rows].astype(F32)
        x_out[i] = far.astype(BF16)
        send(x_out.at[i], x_recv.at[i], pxs.at[i], pxr.at[i], x_to)
    for i in (0, 1):
        near = part[0, i, own_rows] + b_recv[0, i, own_rows].astype(F32) + b_recv[1, i, own_rows].astype(F32)
        arrive(x_recv.at[i], pxr.at[i])
        out_ref[i] = (near + x_recv[i].astype(F32)).astype(BF16)
    for copy in started:
        copy.wait_send()


def own_gamma(factors, occ_energy, vir_energy):
    occupied, rows, width = factors.shape
    nz, nyx = lax.axis_size("z"), lax.axis_size(ROW)
    group = rows * nyx
    row_e = lax.dynamic_slice_in_dim(vir_energy, lax.axis_index("z") * group, group).reshape(group, 1)
    col_e = lax.dynamic_index_in_dim(
        vir_energy.reshape(nz, nyx, rows), lax.axis_index(ROW), 1, keepdims=False
    ).reshape(1, group)
    half = group // 2
    dma = pltpu.SemaphoreType.DMA
    vmem = pl.BlockSpec(memory_space=pltpu.VMEM)
    smem = pl.BlockSpec(memory_space=pltpu.SMEM)
    sems = [(2, 4, 2)] * 2 + [(2, 4)] * 2 + [(6,)] * 2 + [(2,)] * 8 + [(2, 2)] * 2 + [(2,)] * 2
    return pl.pallas_call(
        gamma_kernel,
        out_shape=jax.ShapeDtypeStruct((occupied, rows, width), BF16),
        in_specs=[vmem, smem, vmem, vmem],
        out_specs=vmem,
        scratch_shapes=[
            pltpu.VMEM((2, nyx, rows, width), BF16),
            pltpu.VMEM((2, nz, rows, width), BF16),
            pltpu.VMEM((2, half, 2 * group), F32),
            pltpu.VMEM((2, half, 2 * group), F32),
            pltpu.VMEM((2, half, 2 * group), F32),
            pltpu.VMEM((2, half, 2 * group), BF16),
            pltpu.VMEM((2, half, 2 * group), BF16),
            pltpu.VMEM((2, group, 2 * group), BF16),
            pltpu.VMEM((3, 2, 2 * rows, width), F32),
            pltpu.VMEM((2, 2 * rows, width), BF16),
            pltpu.VMEM((2, 2 * rows, width), BF16),
            pltpu.VMEM((2, 2, 2 * rows, width), BF16),
            pltpu.VMEM((2, 2, 2 * rows, width), BF16),
            pltpu.VMEM((2, rows, width), BF16),
            pltpu.VMEM((2, rows, width), BF16),
        ] + [dma(s) for s in sems],
        compiler_params=pltpu.CompilerParams(
            collective_id=0, has_side_effects=True, vmem_limit_bytes=56 * 1024 * 1024
        ),
        name="own_gamma",
    )(factors, occ_energy, row_e, col_e)


def per_device(factors, occ_energy, vir_energy, block_lengths, block_owner):
    occupied, rows, width = factors.shape
    owners = lax.axis_size("z") * lax.axis_size(ROW)
    capacity = 8 * width // (3 * owners)
    quarter = lax.axis_index(VIR)
    lengths = lax.dynamic_index_in_dim(block_lengths, quarter, 0, keepdims=False)
    owner_of = lax.dynamic_index_in_dim(block_owner, quarter, 0, keepdims=False)
    order = jnp.arange(owners, dtype=jnp.int32)
    starts = jnp.sum(jnp.where(order[None, :] < order[:, None], lengths[None, :], 0), axis=1)
    match = owner_of[None, :] == order[:, None]
    dest_start = jnp.sum(jnp.where(match, starts[None, :], 0), axis=1)
    dest_length = jnp.sum(jnp.where(match, lengths[None, :], 0), axis=1)
    slot = jnp.arange(capacity, dtype=jnp.int32)
    columns = jnp.where(slot[None, :] < dest_length[:, None], dest_start[:, None] + slot[None, :], -1)
    gamma = own_gamma(factors, occ_energy, vir_energy)
    chosen = (columns.reshape(-1)[:, None] == jnp.arange(width, dtype=jnp.int32)[None, :]).astype(BF16)
    picked = jnp.einsum("sp,iap->sia", chosen, gamma, preferred_element_type=F32).astype(BF16)
    outgoing = picked.reshape(owners, capacity * occupied * rows)
    incoming = lax.all_to_all(outgoing, ("z",) + ROW, split_axis=0, concat_axis=0, tiled=True)
    incoming = incoming.reshape(owners, capacity, occupied, rows)
    return jnp.transpose(incoming, (1, 2, 0, 3)).reshape(capacity, occupied, owners * rows)


def solution(mesh):
    fine = Mesh(mesh.devices.reshape(8, 4, 2, 2, 2), ("z", "y", "xl", "xh", "core"))
    placed = (P(None, ("z", "y", "xl"), VIR), P(), P(), P(), P())
    return jax.shard_map(
        per_device,
        mesh=fine,
        in_specs=placed,
        out_specs=P(("z", "y", "xl", "xh", "core"), None, None),
        check_vma=False,
    )
```

```python
import jax
import jax.numpy as jnp
from jax import lax
from jax.experimental import pallas as pl
from jax.experimental.pallas import tpu as pltpu
from jax.sharding import Mesh, PartitionSpec as P

ROW = ("y", "xl")
VIR = ("xh", "core")
F32 = jnp.float32
BF16 = jnp.bfloat16


def ring(axis, shift):
    n = lax.axis_size(axis)
    return lax.rem(lax.axis_index(axis) + shift + n, n)


def flip(axis):
    return 1 - lax.axis_index(axis)


def gamma_kernel(
    f_ref, occ_ref, row_e_ref, col_e_ref, cols_ref, out_ref,
    rbuf, cbuf, m_send, m_own, m_recv, h_send, h_recv, abuf, part,
    a_send, a_recv, b_send, b_recv, x_out, x_recv,
    hop, chosen, gamma, pick_out, pick_in, turned,
    zs, zr, ys, yr, xs, xr, ms, mr, hs, hr, as_, ar, pas, par, pbs, pbr, pxs, pxr,
    rs, rr, qs, qr, ts, tr,
):
    z, y, xl, xh, core = (lax.axis_index(n) for n in ("z", "y", "xl", "xh", "core"))
    rows = f_ref.shape[1]
    width = f_ref.shape[2]

    barrier = pltpu.get_barrier_semaphore()
    yx_steps = [(2, True), (2, False), (1, True), (-1, True), (1, False), (-1, False), (0, True)]
    yx_peers = [{"y": ring("y", dy), "xl": flip("xl") if other else xl} for dy, other in yx_steps]
    z_steps = (4, 3, -3, 2, -2, 1, -1)
    z_peers = [{"z": ring("z", dz)} for dz in z_steps]
    core_to = {"core": flip("core")}
    pair_to = {"xl": flip("xl")}
    cross_to = {"xh": flip("xh"), "xl": flip("xl")}
    xh_to = {"xh": flip("xh")}
    peers = yx_peers + z_peers + [core_to, cross_to, xh_to]
    for peer in peers:
        pl.semaphore_signal(barrier, inc=1, device_id=peer, device_id_type=pl.DeviceIdType.MESH)
    pl.semaphore_wait(barrier, len(peers))

    started = []

    def send(src, dst, ssem, rsem, peer):
        copy = pltpu.make_async_remote_copy(
            src_ref=src, dst_ref=dst, send_sem=ssem, recv_sem=rsem,
            device_id=peer, device_id_type=pl.DeviceIdType.MESH,
        )
        copy.start()
        started.append(copy)
        return copy

    def arrive(dst, rsem):
        pltpu.make_async_remote_copy(
            src_ref=dst, dst_ref=dst, send_sem=rsem, recv_sem=rsem,
            device_id=peers[0], device_id_type=pl.DeviceIdType.MESH,
        ).wait_recv()

    def yx(dy, other):
        return ring("y", dy) * 2 + (flip("xl") if other else xl)

    z_to = ({"z": ring("z", 1)}, {"z": ring("z", -1)})
    y_to = ({"y": ring("y", 1)}, {"y": ring("y", -1)})
    x_to = {"xl": flip("xl")}

    def z_send(d, step, i):
        origin = ring("z", (1 - step) if d == 0 else (step - 1))
        src = f_ref.at[i] if step == 1 else cbuf.at[i, origin]
        send(src, cbuf.at[i, origin], zs.at[d, step - 1, i], zr.at[d, step - 1, i], z_to[d])

    def z_arrive(d, step, i):
        origin = ring("z", -step if d == 0 else step)
        arrive(cbuf.at[i, origin], zr.at[d, step - 1, i])

    def y_send(d, k, i, dy, other):
        src = f_ref.at[i] if (dy == 0 and not other) else rbuf.at[i, yx(dy, other)]
        send(src, rbuf.at[i, yx(dy, other)], ys.at[d, k], yr.at[d, k], y_to[d])

    def y_arrive(d, k, i, dy, other):
        arrive(rbuf.at[i, yx(dy, other)], yr.at[d, k])

    def x_send(k, i, dy):
        src = f_ref.at[i] if dy == 0 else rbuf.at[i, yx(dy, False)]
        send(src, rbuf.at[i, yx(dy, False)], xs.at[k], xr.at[k], x_to)

    def x_arrive(k, i, dy):
        arrive(rbuf.at[i, yx(dy, True)], xr.at[k])

    for i in (0, 1):
        for d in (0, 1):
            z_send(d, 1, i)
            y_send(d, i, i, 0, False)
        x_send(i, i, 0)
    for i in (0, 1):
        cbuf[i, z] = f_ref[i]
        rbuf[i, yx(0, False)] = f_ref[i]
    def choose(step, carry):
        block = step // 6
        first = pl.multiple_of(lax.rem(step, 6) * (width // 6), width // 6)
        at = lax.broadcasted_iota(jnp.int32, (width // 6, cols_ref.shape[2]), 0) + first
        hit = at == cols_ref[block]
        chosen[block, pl.ds(first, width // 6), :] = jnp.where(hit, 1.0, 0.0).astype(BF16)
        return carry

    lax.fori_loop(0, 8 * 6, choose, 0)
    for d in (0, 1):
        z_arrive(d, 1, 0)
        z_send(d, 2, 0)
    y_arrive(0, 0, 0, -1, False)
    x_send(2, 0, -1)
    y_send(0, 2, 0, -1, False)
    y_arrive(1, 0, 0, 1, False)
    for d in (0, 1):
        z_arrive(d, 1, 1)
        z_send(d, 2, 1)
    y_arrive(1, 1, 1, 1, False)
    x_send(3, 1, 1)
    y_send(1, 2, 1, 1, False)
    x_send(4, 0, 1)
    y_arrive(0, 1, 1, -1, False)
    x_send(5, 1, -1)
    for d in (0, 1):
        z_arrive(d, 2, 0)
        z_send(d, 3, 0)
    x_arrive(0, 0, 0)
    x_arrive(1, 1, 0)
    x_arrive(2, 0, -1)
    y_send(0, 3, 0, -1, True)
    for d in (0, 1):
        z_arrive(d, 2, 1)
        z_send(d, 3, 1)
    x_arrive(3, 1, 1)
    y_send(1, 3, 1, 1, True)
    z_arrive(0, 3, 0)
    z_send(0, 4, 0)
    z_arrive(1, 3, 1)
    z_send(1, 4, 1)
    z_arrive(1, 3, 0)
    z_arrive(0, 3, 1)
    y_arrive(0, 2, 0, -2, False)
    y_arrive(1, 2, 1, 2, False)
    x_arrive(4, 0, 1)
    x_arrive(5, 1, -1)
    y_arrive(0, 3, 0, -2, True)
    y_arrive(1, 3, 1, 2, True)
    z_arrive(0, 4, 0)
    z_arrive(1, 4, 1)

    half = 4 * rows
    side = 8 * rows
    columns = cbuf[...].reshape(2 * side, width)

    def pair_rows(i, h):
        lhs = rbuf[i, pl.ds(h * 4, 4)].reshape(half, width)
        return lax.dot_general(lhs, columns, (((1,), (1,)), ((), ())), preferred_element_type=F32)

    for i in (0, 1):
        m_send[i] = pair_rows(i, 1 - core)
        send(m_send.at[i], m_recv.at[i], ms.at[i], mr.at[i], core_to)
    for i in (0, 1):
        m_own[i] = pair_rows(i, core)
    for i in (0, 1):
        arrive(m_recv.at[i], mr.at[i])
        total = m_own[i] + m_recv[i]
        m_own[i] = total
        h_send[i] = total.astype(BF16)
        send(h_send.at[i], hop.at[i], hs.at[i], hr.at[i], (pair_to, cross_to)[i])
    for i in (0, 1):
        arrive(hop.at[i], hr.at[i])
        send(hop.at[i], h_recv.at[i], rs.at[i], rr.at[i], (cross_to, pair_to)[i])
    for i in (0, 1):
        arrive(h_recv.at[i], rr.at[i])
        m_own[i] = m_own[i] + h_recv[i].astype(F32)
    row_e = row_e_ref[pl.ds(pl.multiple_of(core * half, 16), half), :]
    col_e = col_e_ref[...]
    mine = pl.ds(pl.multiple_of(core * half, 16), half)
    for i in (0, 1):
        for j in (0, 1):
            denominator = (occ_ref[i] + occ_ref[j]) - row_e - col_e
            direct = m_own[i, :, pl.ds(j * side, side)]
            swapped = m_own[j, :, pl.ds(i * side, side)]
            abuf[i, mine, pl.ds(j * side, side)] = ((2.0 * direct - swapped) / denominator).astype(BF16)
        send(abuf.at[i, mine], abuf.at[i, mine], as_.at[i], ar.at[i], core_to)
    theirs = pl.ds(pl.multiple_of((1 - core) * half, 16), half)
    for i in (0, 1):
        arrive(abuf.at[i, theirs], ar.at[i])

    pair_rows2 = 2 * rows

    def partial(slot, dy):
        at = pl.ds(pl.multiple_of(ring("y", dy) * pair_rows2, 16), pair_rows2)
        lhs = abuf[:, at, :].reshape(2 * pair_rows2, 2 * side)
        res = jnp.dot(lhs, cbuf[...].reshape(2 * side, width), preferred_element_type=F32)
        part[slot] = res.reshape(2, pair_rows2, width)

    partial(0, 2)
    for d in (0, 1):
        a_send[d] = part[0, d].astype(BF16)
        send(a_send.at[d], a_recv.at[d], pas.at[d], par.at[d], y_to[d])
    for d in (0, 1):
        partial(1 + d, 1 if d == 0 else -1)
        i = 1 - d
        b_send[d, i] = part[1 + d, i].astype(BF16)
        send(b_send.at[d, i], b_recv.at[d, i], pbs.at[d, i], pbr.at[d, i], y_to[d])
    for d in (0, 1):
        arrive(a_recv.at[d], par.at[d])
        b_send[d, d] = (part[1 + d, d] + a_recv[d].astype(F32)).astype(BF16)
        send(b_send.at[d, d], b_recv.at[d, d], pbs.at[d, d], pbr.at[d, d], y_to[d])
    partial(0, 0)
    own_rows = pl.ds(pl.multiple_of(xl * rows, 16), rows)
    far_rows = pl.ds(pl.multiple_of((1 - xl) * rows, 16), rows)
    for i in (0, 1):
        for d in (0, 1):
            arrive(b_recv.at[d, i], pbr.at[d, i])
        far = part[0, i, far_rows] + b_recv[0, i, far_rows].astype(F32) + b_recv[1, i, far_rows].astype(F32)
        x_out[i] = far.astype(BF16)
        send(x_out.at[i], x_recv.at[i], pxs.at[i], pxr.at[i], x_to)
    for i in (0, 1):
        near = part[0, i, own_rows] + b_recv[0, i, own_rows].astype(F32) + b_recv[1, i, own_rows].astype(F32)
        arrive(x_recv.at[i], pxr.at[i])
        gamma[pl.ds(i * rows, rows), :] = (near + x_recv[i].astype(F32)).astype(BF16)

    slots = cols_ref.shape[2]
    me = yx(0, False)

    def picked(block):
        got = jnp.dot(gamma[...], chosen[block], preferred_element_type=F32)
        return got.astype(BF16).reshape(2, rows, slots)

    for k, (dy, other) in enumerate(yx_steps):
        pick_out[k] = picked(yx(dy, other))
        send(pick_out.at[k], pick_in.at[:, me], qs.at[k], qr.at[k], yx_peers[k])
    pick_in[:, me] = picked(me)
    for k, (dy, other) in enumerate(yx_steps):
        arrive(pick_in.at[:, yx(-dy, other)], qr.at[k])
    for c in range(slots // 128):
        block = pick_in[:, :, :, pl.ds(c * 128, 128)].reshape(2 * side, 128)
        turned[pl.ds(c * 128, 128), :] = block.astype(F32).T.astype(BF16)
    capacity = slots // 8

    def owner_rows(dz):
        return turned.at[pl.ds(pl.multiple_of(ring("z", dz) * capacity, 16), capacity)]

    for k, dz in enumerate(z_steps):
        send(owner_rows(dz), out_ref.at[z], ts.at[k], tr.at[k], z_peers[k])
    out_ref[z] = owner_rows(0)[...]
    for k, dz in enumerate(z_steps):
        arrive(out_ref.at[ring("z", -dz)], tr.at[k])
    for copy in started:
        copy.wait_send()


def owned_columns(factors, occ_energy, vir_energy, columns):
    occupied, rows, width = factors.shape
    nz, nyx = lax.axis_size("z"), lax.axis_size(ROW)
    group = rows * nyx
    row_e = lax.dynamic_slice_in_dim(vir_energy, lax.axis_index("z") * group, group).reshape(group, 1)
    col_e = lax.dynamic_index_in_dim(
        vir_energy.reshape(nz, nyx, rows), lax.axis_index(ROW), 1, keepdims=False
    ).reshape(1, group)
    half = group // 2
    dma = pltpu.SemaphoreType.DMA
    vmem = pl.BlockSpec(memory_space=pltpu.VMEM)
    smem = pl.BlockSpec(memory_space=pltpu.SMEM)
    sems = [(2, 4, 2)] * 2 + [(2, 4)] * 2 + [(6,)] * 2 + [(2,)] * 8 + [(2, 2)] * 2 + [(2,)] * 4 + [(7,)] * 4
    slots = columns.shape[1]
    return pl.pallas_call(
        gamma_kernel,
        out_shape=jax.ShapeDtypeStruct((nz, slots // nz, 2 * group), BF16),
        in_specs=[vmem, smem, vmem, vmem, vmem],
        out_specs=vmem,
        scratch_shapes=[
            pltpu.VMEM((2, nyx, rows, width), BF16),
            pltpu.VMEM((2, nz, rows, width), BF16),
            pltpu.VMEM((2, half, 2 * group), F32),
            pltpu.VMEM((2, half, 2 * group), F32),
            pltpu.VMEM((2, half, 2 * group), F32),
            pltpu.VMEM((2, half, 2 * group), BF16),
            pltpu.VMEM((2, half, 2 * group), BF16),
            pltpu.VMEM((2, group, 2 * group), BF16),
            pltpu.VMEM((3, 2, 2 * rows, width), F32),
            pltpu.VMEM((2, 2 * rows, width), BF16),
            pltpu.VMEM((2, 2 * rows, width), BF16),
            pltpu.VMEM((2, 2, 2 * rows, width), BF16),
            pltpu.VMEM((2, 2, 2 * rows, width), BF16),
            pltpu.VMEM((2, rows, width), BF16),
            pltpu.VMEM((2, rows, width), BF16),
            pltpu.VMEM((2, half, 2 * group), BF16),
            pltpu.VMEM((nyx, width, slots), BF16),
            pltpu.VMEM((2 * rows, width), BF16),
            pltpu.VMEM((7, 2, rows, slots), BF16),
            pltpu.VMEM((2, nyx, rows, slots), BF16),
            pltpu.VMEM((slots, 2 * group), BF16),
        ] + [dma(s) for s in sems],
        compiler_params=pltpu.CompilerParams(
            collective_id=0, has_side_effects=True, vmem_limit_bytes=56 * 1024 * 1024
        ),
        name="owned_columns",
    )(factors, occ_energy, row_e, col_e, columns.reshape(nyx, 1, slots))


def per_device(factors, occ_energy, vir_energy, block_lengths, block_owner):
    occupied, rows, width = factors.shape
    owners = lax.axis_size("z") * lax.axis_size(ROW)
    capacity = 8 * width // (3 * owners)
    quarter = lax.axis_index(VIR)
    lengths = lax.dynamic_index_in_dim(block_lengths, quarter, 0, keepdims=False)
    owner_of = lax.dynamic_index_in_dim(block_owner, quarter, 0, keepdims=False)
    order = jnp.arange(owners, dtype=jnp.int32)
    starts = jnp.sum(jnp.where(order[None, :] < order[:, None], lengths[None, :], 0), axis=1)
    match = owner_of[None, :] == order[:, None]
    dest_start = jnp.sum(jnp.where(match, starts[None, :], 0), axis=1)
    dest_length = jnp.sum(jnp.where(match, lengths[None, :], 0), axis=1)
    slot = jnp.arange(capacity, dtype=jnp.int32)
    columns = jnp.where(slot[None, :] < dest_length[:, None], dest_start[:, None] + slot[None, :], -1)
    nz, nyx = lax.axis_size("z"), lax.axis_size(ROW)
    columns = jnp.transpose(columns.reshape(nz, nyx, capacity), (1, 0, 2)).reshape(nyx, nz * capacity)
    got = owned_columns(factors, occ_energy, vir_energy, columns)
    got = got.reshape(nz, capacity, occupied, nyx * rows)
    return jnp.transpose(got, (1, 2, 0, 3)).reshape(capacity, occupied, owners * rows)


def solution(mesh):
    fine = Mesh(mesh.devices.reshape(8, 4, 2, 2, 2), ("z", "y", "xl", "xh", "core"))
    placed = (P(None, ("z", "y", "xl"), VIR), P(), P(), P(), P())
    return jax.shard_map(
        per_device,
        mesh=fine,
        in_specs=placed,
        out_specs=P(("z", "y", "xl", "xh", "core"), None, None),
        check_vma=False,
    )
```

```python
import jax
import jax.numpy as jnp
from jax import lax
from jax.experimental import pallas as pl
from jax.experimental.pallas import tpu as pltpu
from jax.sharding import Mesh, PartitionSpec as P

ROW = ("y", "xl")
VIR = ("xh", "core")
F32 = jnp.float32
BF16 = jnp.bfloat16


def ring(axis, shift):
    n = lax.axis_size(axis)
    return lax.rem(lax.axis_index(axis) + shift + n, n)


def flip(axis):
    return 1 - lax.axis_index(axis)


def gamma_kernel(
    f_ref, occ_ref, vir_ref, start_ref, length_ref, out_ref,
    rbuf, cbuf, m_send, m_own, m_recv, h_send, h_recv, hop, abuf, part, row_e_buf,
    ya_out, ya_in, yb_out, yb_in, yc_out, yc_in, xa_out, xa_in, xb_out, xb_in, xc_out, xc_in,
    chosen, gamma, pick_out, pick_in, turned,
    zs, zr, ys, yr, xs, xr, ms, mr, hs, hr, rs, rr, as_, ar,
    yas, yar, ybs, ybr, ycs, ycr, xas, xar, xbs, xbr, xcs, xcr, qs, qr, ts, tr,
):
    z, y, xl, xh, core = (lax.axis_index(n) for n in ("z", "y", "xl", "xh", "core"))
    rows = f_ref.shape[1]
    width = f_ref.shape[2]

    barrier = pltpu.get_barrier_semaphore()
    yx_steps = [(2, True), (2, False), (1, True), (-1, True), (1, False), (-1, False), (0, True)]
    yx_peers = [{"y": ring("y", dy), "xl": flip("xl") if other else xl} for dy, other in yx_steps]
    z_steps = (4, 3, -3, 2, -2, 1, -1)
    z_peers = [{"z": ring("z", dz)} for dz in z_steps]
    core_to = {"core": flip("core")}
    pair_to = {"xl": flip("xl")}
    cross_to = {"xh": flip("xh"), "xl": flip("xl")}
    xh_to = {"xh": flip("xh")}
    peers = yx_peers + z_peers + [core_to, cross_to, xh_to]
    for peer in peers:
        pl.semaphore_signal(barrier, inc=1, device_id=peer, device_id_type=pl.DeviceIdType.MESH)
    pl.semaphore_wait(barrier, len(peers))

    started = []

    def send(src, dst, ssem, rsem, peer):
        copy = pltpu.make_async_remote_copy(
            src_ref=src, dst_ref=dst, send_sem=ssem, recv_sem=rsem,
            device_id=peer, device_id_type=pl.DeviceIdType.MESH,
        )
        copy.start()
        started.append(copy)
        return copy

    def arrive(dst, rsem):
        pltpu.make_async_remote_copy(
            src_ref=dst, dst_ref=dst, send_sem=rsem, recv_sem=rsem,
            device_id=peers[0], device_id_type=pl.DeviceIdType.MESH,
        ).wait_recv()

    def yx(dy, other):
        return ring("y", dy) * 2 + (flip("xl") if other else xl)

    z_to = ({"z": ring("z", 1)}, {"z": ring("z", -1)})
    y_to = ({"y": ring("y", 1)}, {"y": ring("y", -1)})
    x_to = {"xl": flip("xl")}

    def z_send(d, step, i):
        origin = ring("z", (1 - step) if d == 0 else (step - 1))
        src = f_ref.at[i] if step == 1 else cbuf.at[i, origin]
        send(src, cbuf.at[i, origin], zs.at[d, step - 1, i], zr.at[d, step - 1, i], z_to[d])

    def z_arrive(d, step, i):
        origin = ring("z", -step if d == 0 else step)
        arrive(cbuf.at[i, origin], zr.at[d, step - 1, i])

    def y_send(d, k, i, dy, other):
        src = f_ref.at[i] if (dy == 0 and not other) else rbuf.at[i, yx(dy, other)]
        send(src, rbuf.at[i, yx(dy, other)], ys.at[d, k], yr.at[d, k], y_to[d])

    def y_arrive(d, k, i, dy, other):
        arrive(rbuf.at[i, yx(dy, other)], yr.at[d, k])

    def x_send(k, i, dy):
        src = f_ref.at[i] if dy == 0 else rbuf.at[i, yx(dy, False)]
        send(src, rbuf.at[i, yx(dy, False)], xs.at[k], xr.at[k], x_to)

    def x_arrive(k, i, dy):
        arrive(rbuf.at[i, yx(dy, True)], xr.at[k])

    for i in (0, 1):
        for d in (0, 1):
            z_send(d, 1, i)
            y_send(d, i, i, 0, False)
        x_send(i, i, 0)
    for i in (0, 1):
        cbuf[i, z] = f_ref[i]
        rbuf[i, yx(0, False)] = f_ref[i]
    slots = chosen.shape[2]
    capacity = slots // 8
    piece = width // 6

    def choose(block, carry):
        lane = lax.broadcasted_iota(jnp.int32, (1, slots), 1)
        first = jnp.zeros((1, slots), jnp.int32)
        count = jnp.zeros((1, slots), jnp.int32)
        for zt in range(8):
            here = lane // capacity == zt
            first = jnp.where(here, start_ref[zt * 8 + block], first)
            count = jnp.where(here, length_ref[zt * 8 + block], count)
        slot = lane % capacity
        column = jnp.where(slot < count, first + slot, -1)
        for k in range(6):
            at = lax.broadcasted_iota(jnp.int32, (piece, slots), 0) + k * piece
            chosen[block, pl.ds(k * piece, piece), :] = jnp.where(at == column, 1.0, 0.0).astype(BF16)
        return carry

    lax.fori_loop(0, 8, choose, 0)
    near_e = jnp.concatenate([vir_ref[pl.ds(z * 8 + k, 1), :] for k in range(8)], axis=1)
    row_e_buf[...] = jnp.broadcast_to(near_e, (128, 8 * rows)).T
    col_e = jnp.concatenate([vir_ref[pl.ds(k * 8 + yx(0, False), 1), :] for k in range(8)], axis=1)
    for d in (0, 1):
        z_arrive(d, 1, 0)
        z_send(d, 2, 0)
    y_arrive(0, 0, 0, -1, False)
    x_send(2, 0, -1)
    y_send(0, 2, 0, -1, False)
    y_arrive(1, 0, 0, 1, False)
    for d in (0, 1):
        z_arrive(d, 1, 1)
        z_send(d, 2, 1)
    y_arrive(1, 1, 1, 1, False)
    x_send(3, 1, 1)
    y_send(1, 2, 1, 1, False)
    x_send(4, 0, 1)
    y_arrive(0, 1, 1, -1, False)
    x_send(5, 1, -1)
    for d in (0, 1):
        z_arrive(d, 2, 0)
        z_send(d, 3, 0)
    x_arrive(0, 0, 0)
    x_arrive(1, 1, 0)
    x_arrive(2, 0, -1)
    y_send(0, 3, 0, -1, True)
    for d in (0, 1):
        z_arrive(d, 2, 1)
        z_send(d, 3, 1)
    x_arrive(3, 1, 1)
    y_send(1, 3, 1, 1, True)
    z_arrive(0, 3, 0)
    z_send(0, 4, 0)
    z_arrive(1, 3, 1)
    z_send(1, 4, 1)
    z_arrive(1, 3, 0)
    z_arrive(0, 3, 1)
    y_arrive(0, 2, 0, -2, False)
    y_arrive(1, 2, 1, 2, False)
    x_arrive(4, 0, 1)
    x_arrive(5, 1, -1)
    y_arrive(0, 3, 0, -2, True)
    y_arrive(1, 3, 1, 2, True)
    z_arrive(0, 4, 0)
    z_arrive(1, 4, 1)

    half = 4 * rows
    side = 8 * rows
    columns = cbuf[...].reshape(2 * side, width)

    def pair_rows(i, h):
        lhs = rbuf[i, pl.ds(h * 4, 4)].reshape(half, width)
        return lax.dot_general(lhs, columns, (((1,), (1,)), ((), ())), preferred_element_type=F32)

    for i in (0, 1):
        m_send[i] = pair_rows(i, 1 - core)
        send(m_send.at[i], m_recv.at[i], ms.at[i], mr.at[i], core_to)
    for i in (0, 1):
        m_own[i] = pair_rows(i, core)
    for i in (0, 1):
        arrive(m_recv.at[i], mr.at[i])
        total = m_own[i] + m_recv[i]
        m_own[i] = total
        h_send[i] = total.astype(BF16)
        send(h_send.at[i], hop.at[i], hs.at[i], hr.at[i], (pair_to, cross_to)[i])
    for i in (0, 1):
        arrive(hop.at[i], hr.at[i])
        send(hop.at[i], h_recv.at[i], rs.at[i], rr.at[i], (cross_to, pair_to)[i])
    for i in (0, 1):
        arrive(h_recv.at[i], rr.at[i])
        m_own[i] = m_own[i] + h_recv[i].astype(F32)
    row_e = row_e_buf[pl.ds(pl.multiple_of(core * half, 16), half), 0:1]
    mine = pl.ds(pl.multiple_of(core * half, 16), half)
    for i in (0, 1):
        for j in (0, 1):
            denominator = (occ_ref[i] + occ_ref[j]) - row_e - col_e
            direct = m_own[i, :, pl.ds(j * side, side)]
            swapped = m_own[j, :, pl.ds(i * side, side)]
            abuf[i, mine, pl.ds(j * side, side)] = ((2.0 * direct - swapped) / denominator).astype(BF16)
        send(abuf.at[i, mine], abuf.at[i, mine], as_.at[i], ar.at[i], core_to)
    theirs = pl.ds(pl.multiple_of((1 - core) * half, 16), half)
    for i in (0, 1):
        arrive(abuf.at[i, theirs], ar.at[i])

    cols = width // 2
    quad = cols // 2
    me = yx(0, False)
    mate = yx(0, True)
    left, right = pl.ds(0, cols), pl.ds(cols, cols)

    def wide(ref):
        return ref[...].astype(F32)

    def product(i):
        for h in (0, 1):
            lhs = abuf[i, pl.ds(h * half, half)]
            res = jnp.dot(lhs, cbuf[...].reshape(2 * side, width), preferred_element_type=F32)
            part[i, pl.ds(4 * h, 4)] = res.reshape(4, rows, width)

    def s1(i):
        for d in (0, 1):
            ya_out[i, d] = part[i, ring("y", 2) * 2 + d, :, left].astype(BF16)
            send(ya_out.at[i, d], ya_in.at[i, d], yas.at[i, d], yar.at[i, d], y_to[d])
        for k, dy in enumerate((2, 1, -1, 0)):
            xa_out[i, k] = part[i, yx(dy, True), :, right].astype(BF16)
            send(xa_out.at[i, k], xa_in.at[i, k], xas.at[i, k], xar.at[i, k], x_to)
        for d in (0, 1):
            yb_send(i, d, 1 - d, part[i, ring("y", 1 - 2 * d) * 2 + 1 - d, :, left])

    def yb_send(i, d, e, value):
        yb_out[i, d, e] = value.astype(BF16)
        send(yb_out.at[i, d, e], yb_in.at[i, d, e], ybs.at[i, d, e], ybr.at[i, d, e], y_to[d])

    def s2(i):
        for d in (0, 1):
            arrive(ya_in.at[i, d], yar.at[i, d])
            yb_send(i, d, d, part[i, ring("y", 1 - 2 * d) * 2 + d, :, left] + wide(ya_in.at[i, d]))

    def xc_send(i, d, e, value):
        xc_out[i, d, e] = value.astype(BF16)
        send(xc_out.at[i, d, e], xc_in.at[i, d, e], xcs.at[i, d, e], xcr.at[i, d, e], y_to[d])

    def x_sum(i, k, dy, e):
        at = pl.ds(cols + e * quad, quad)
        return part[i, yx(dy, False), :, at] + xa_in[i, k, :, pl.ds(e * quad, quad)].astype(F32)

    def s3(i):
        arrive(xa_in.at[i, 0], xar.at[i, 0])
        for d in (0, 1):
            xb_out[i, d] = x_sum(i, 0, 2, d).astype(BF16)
            send(xb_out.at[i, d], xb_in.at[i, d], xbs.at[i, d], xbr.at[i, d], y_to[d])
        for d in (0, 1):
            arrive(xa_in.at[i, 1 + d], xar.at[i, 1 + d])
            xc_send(i, d, 1 - d, x_sum(i, 1 + d, 1 - 2 * d, 1 - d))

    def s4(i):
        for d in (0, 1):
            arrive(xb_in.at[i, d], xbr.at[i, d])
            xc_send(i, d, d, x_sum(i, 1 + d, 1 - 2 * d, d) + wide(xb_in.at[i, d]))

    def s5(i):
        for d in (0, 1):
            for e in (1 - d, d):
                arrive(yb_in.at[i, d, e], ybr.at[i, d, e])
        far = part[i, mate, :, left] + wide(yb_in.at[i, 0, 1 - xl]) + wide(yb_in.at[i, 1, 1 - xl])
        yc_out[i] = far.astype(BF16)
        send(yc_out.at[i], yc_in.at[i], ycs.at[i], ycr.at[i], x_to)

    def s6(i):
        arrive(xa_in.at[i, 3], xar.at[i, 3])
        for d in (0, 1):
            for e in (1 - d, d):
                arrive(xc_in.at[i, d, e], xcr.at[i, d, e])
        for e in (0, 1):
            total = x_sum(i, 3, 0, e) + wide(xc_in.at[i, 0, e]) + wide(xc_in.at[i, 1, e])
            gamma[i, :, pl.ds(cols + e * quad, quad)] = total.astype(BF16)
        near = part[i, me, :, left] + wide(yb_in.at[i, 0, xl]) + wide(yb_in.at[i, 1, xl])
        arrive(yc_in.at[i], ycr.at[i])
        gamma[i, :, left] = (near + wide(yc_in.at[i])).astype(BF16)

    def picked(i, block):
        return jnp.dot(gamma[i], chosen[block], preferred_element_type=F32).astype(BF16)

    def s7(i):
        for k, (dy, other) in enumerate(yx_steps):
            pick_out[i, k] = picked(i, yx(dy, other))
            send(pick_out.at[i, k], pick_in.at[i, me], qs.at[i, k], qr.at[i, k], yx_peers[k])
        pick_in[i, me] = picked(i, me)

    def owner_rows(i, dz):
        return turned.at[i, pl.ds(pl.multiple_of(ring("z", dz) * capacity, 16), capacity)]

    def s8(i):
        for k, (dy, other) in enumerate(yx_steps):
            arrive(pick_in.at[i, yx(-dy, other)], qr.at[i, k])
        for c in range(slots // 128):
            block = pick_in[i, :, :, pl.ds(c * 128, 128)].reshape(side, 128)
            turned[i, pl.ds(c * 128, 128), :] = block.astype(F32).T.astype(BF16)
        for k, dz in enumerate(z_steps):
            send(owner_rows(i, dz), out_ref.at[i, z], ts.at[i, k], tr.at[i, k], z_peers[k])
        out_ref[i, z] = owner_rows(i, 0)[...]

    def s9(i):
        for k, dz in enumerate(z_steps):
            arrive(out_ref.at[i, ring("z", -dz)], tr.at[i, k])

    product(0)
    s1(0)
    product(1)
    s2(0)
    s3(0)
    s1(1)
    s4(0)
    s5(0)
    s2(1)
    s3(1)
    s6(0)
    s7(0)
    s4(1)
    s5(1)
    s8(0)
    s6(1)
    s7(1)
    s8(1)
    s9(0)
    s9(1)
    for copy in started:
        copy.wait_send()


def owned_columns(factors, occ_energy, vir_energy, start, length):
    occupied, rows, width = factors.shape
    nz, nyx = lax.axis_size("z"), lax.axis_size(ROW)
    group = rows * nyx
    half = group // 2
    slots = 8 * width // (3 * nyx)
    cols = width // 2
    dma = pltpu.SemaphoreType.DMA
    vmem = pl.BlockSpec(memory_space=pltpu.VMEM)
    smem = pl.BlockSpec(memory_space=pltpu.SMEM)
    wide = [pltpu.VMEM((2, half, 2 * group), F32)] * 3
    thin = [pltpu.VMEM((2, half, 2 * group), BF16)] * 3

    def pair_of(*shape):
        return [pltpu.VMEM(shape, BF16)] * 2

    sems = [(2, 4, 2)] * 2 + [(2, 4)] * 2 + [(6,)] * 2 + [(2,)] * 8
    sems += [(2, 2)] * 2 + [(2, 2, 2)] * 2 + [(2,)] * 2 + [(2, 4)] * 2 + [(2, 2)] * 2 + [(2, 2, 2)] * 2 + [(2, 7)] * 4
    return pl.pallas_call(
        gamma_kernel,
        out_shape=jax.ShapeDtypeStruct((2, nz, slots // nz, group), BF16),
        in_specs=[vmem, smem, vmem, smem, smem],
        out_specs=vmem,
        scratch_shapes=pair_of(2, 8, rows, width)
        + wide
        + thin
        + [
            pltpu.VMEM((2, group, 2 * group), BF16),
            pltpu.VMEM((2, nyx, rows, width), F32),
            pltpu.VMEM((group, 128), F32),
        ]
        + pair_of(2, 2, rows, cols)
        + pair_of(2, 2, 2, rows, cols)
        + pair_of(2, rows, cols)
        + pair_of(2, 4, rows, cols)
        + pair_of(2, 2, rows, cols // 2)
        + pair_of(2, 2, 2, rows, cols // 2)
        + [
            pltpu.VMEM((nyx, width, slots), BF16),
            pltpu.VMEM((2, rows, width), BF16),
            pltpu.VMEM((2, 7, rows, slots), BF16),
            pltpu.VMEM((2, nyx, rows, slots), BF16),
            pltpu.VMEM((2, slots, group), BF16),
        ]
        + [dma(s) for s in sems],
        compiler_params=pltpu.CompilerParams(
            collective_id=0, has_side_effects=True, vmem_limit_bytes=60 * 1024 * 1024
        ),
        name="owned_columns",
    )(factors, occ_energy, vir_energy.reshape(nz * nyx, rows), start, length)


def per_device(factors, occ_energy, vir_energy, block_lengths, block_owner):
    occupied, rows, width = factors.shape
    nz, nyx = lax.axis_size("z"), lax.axis_size(ROW)
    owners = nz * nyx
    quarter = lax.axis_index(VIR)
    lengths = lax.dynamic_index_in_dim(block_lengths, quarter, 0, keepdims=False)
    owner_of = lax.dynamic_index_in_dim(block_owner, quarter, 0, keepdims=False)
    order = jnp.arange(owners, dtype=jnp.int32)
    starts = jnp.sum(jnp.where(order[None, :] < order[:, None], lengths[None, :], 0), axis=1)
    match = owner_of[None, :] == order[:, None]
    dest_start = jnp.sum(jnp.where(match, starts[None, :], 0), axis=1)
    dest_length = jnp.sum(jnp.where(match, lengths[None, :], 0), axis=1)
    got = owned_columns(factors, occ_energy, vir_energy, dest_start, dest_length)
    return jnp.transpose(got, (2, 0, 1, 3)).reshape(got.shape[2], occupied, owners * rows)


def solution(mesh):
    fine = Mesh(mesh.devices.reshape(8, 4, 2, 2, 2), ("z", "y", "xl", "xh", "core"))
    placed = (P(None, ("z", "y", "xl"), VIR), P(), P(), P(), P())
    return jax.shard_map(
        per_device,
        mesh=fine,
        in_specs=placed,
        out_specs=P(("z", "y", "xl", "xh", "core"), None, None),
        check_vma=False,
    )
```

```python
import jax
import jax.numpy as jnp
from jax import lax
from jax.experimental import pallas as pl
from jax.experimental.pallas import tpu as pltpu
from jax.sharding import Mesh, PartitionSpec as P

ROW = ("y", "xl")
VIR = ("xh", "core")
F32 = jnp.float32
BF16 = jnp.bfloat16


def ring(axis, shift):
    n = lax.axis_size(axis)
    return lax.rem(lax.axis_index(axis) + shift + n, n)


def flip(axis):
    return 1 - lax.axis_index(axis)


def gamma_kernel(
    f_ref, occ_ref, vir_ref, start_ref, length_ref, out_ref,
    rbuf, cbuf, m_send, m_own, m_recv, h_send, h_recv, hop, abuf, part, row_e_buf,
    ya_out, ya_in, yb_out, yb_in, yc_out, yc_in, xa_out, xa_in, xb_out, xb_in, xc_out, xc_in,
    gamma, window, spread, pick_out, pick_in, turned,
    zs, zr, ys, yr, xs, xr, ms, mr, hs, hr, rs, rr, as_, ar,
    yas, yar, ybs, ybr, ycs, ycr, xas, xar, xbs, xbr, xcs, xcr, qs, qr, ts, tr, fs, os_,
):
    z, y, xl, xh, core = (lax.axis_index(n) for n in ("z", "y", "xl", "xh", "core"))
    rows = f_ref.shape[1]
    width = f_ref.shape[2]

    barrier = pltpu.get_barrier_semaphore()
    yx_steps = [(2, True), (2, False), (1, True), (-1, True), (1, False), (-1, False), (0, True)]
    yx_peers = [{"y": ring("y", dy), "xl": flip("xl") if other else xl} for dy, other in yx_steps]
    z_steps = (4, 3, -3, 2, -2, 1, -1)
    z_peers = [{"z": ring("z", dz)} for dz in z_steps]
    core_to = {"core": flip("core")}
    pair_to = {"xl": flip("xl")}
    cross_to = {"xh": flip("xh"), "xl": flip("xl")}
    peers = [z_peers[-2], z_peers[-1], yx_peers[4], yx_peers[5], pair_to, cross_to, core_to]
    for peer in peers:
        pl.semaphore_signal(barrier, inc=1, device_id=peer, device_id_type=pl.DeviceIdType.MESH)
    pl.semaphore_wait(barrier, len(peers))

    started = []

    def send(src, dst, ssem, rsem, peer):
        copy = pltpu.make_async_remote_copy(
            src_ref=src, dst_ref=dst, send_sem=ssem, recv_sem=rsem,
            device_id=peer, device_id_type=pl.DeviceIdType.MESH,
        )
        copy.start()
        started.append(copy)
        return copy

    def arrive(dst, rsem):
        pltpu.make_async_remote_copy(
            src_ref=dst, dst_ref=dst, send_sem=rsem, recv_sem=rsem,
            device_id=peers[0], device_id_type=pl.DeviceIdType.MESH,
        ).wait_recv()

    def yx(dy, other):
        return ring("y", dy) * 2 + (flip("xl") if other else xl)

    z_to = ({"z": ring("z", 1)}, {"z": ring("z", -1)})
    y_to = ({"y": ring("y", 1)}, {"y": ring("y", -1)})
    x_to = {"xl": flip("xl")}

    def z_send(d, step, i):
        origin = ring("z", (1 - step) if d == 0 else (step - 1))
        src = f_ref.at[i] if step == 1 else cbuf.at[i, origin]
        send(src, cbuf.at[i, origin], zs.at[d, step - 1, i], zr.at[d, step - 1, i], z_to[d])

    def z_arrive(d, step, i):
        origin = ring("z", -step if d == 0 else step)
        arrive(cbuf.at[i, origin], zr.at[d, step - 1, i])

    def y_send(d, k, i, dy, other):
        src = f_ref.at[i] if (dy == 0 and not other) else rbuf.at[i, yx(dy, other)]
        send(src, rbuf.at[i, yx(dy, other)], ys.at[d, k], yr.at[d, k], y_to[d])

    def y_arrive(d, k, i, dy, other):
        arrive(rbuf.at[i, yx(dy, other)], yr.at[d, k])

    def x_send(k, i, dy):
        src = f_ref.at[i] if dy == 0 else rbuf.at[i, yx(dy, False)]
        send(src, rbuf.at[i, yx(dy, False)], xs.at[k], xr.at[k], x_to)

    def x_arrive(k, i, dy):
        arrive(rbuf.at[i, yx(dy, True)], xr.at[k])

    for i in (0, 1):
        for d in (0, 1):
            z_send(d, 1, i)
            y_send(d, i, i, 0, False)
        x_send(i, i, 0)
    local = []
    for i in (0, 1):
        local.append(pltpu.make_async_copy(f_ref.at[i], cbuf.at[i, z], fs.at[0, i]))
        local.append(pltpu.make_async_copy(f_ref.at[i], rbuf.at[i, yx(0, False)], fs.at[1, i]))
    for copy in local:
        copy.start()
    near_e = jnp.concatenate([vir_ref[pl.ds(z * 8 + k, 1), :] for k in range(8)], axis=1)
    row_e_buf[...] = jnp.broadcast_to(near_e, (128, 8 * rows)).T
    col_e = jnp.concatenate([vir_ref[pl.ds(k * 8 + yx(0, False), 1), :] for k in range(8)], axis=1)
    for d in (0, 1):
        z_arrive(d, 1, 0)
        z_send(d, 2, 0)
    y_arrive(0, 0, 0, -1, False)
    x_send(2, 0, -1)
    y_send(0, 2, 0, -1, False)
    y_arrive(1, 0, 0, 1, False)
    for d in (0, 1):
        z_arrive(d, 1, 1)
        z_send(d, 2, 1)
    y_arrive(1, 1, 1, 1, False)
    x_send(3, 1, 1)
    y_send(1, 2, 1, 1, False)
    x_send(4, 0, 1)
    y_arrive(0, 1, 1, -1, False)
    x_send(5, 1, -1)
    for d in (0, 1):
        z_arrive(d, 2, 0)
        z_send(d, 3, 0)
    x_arrive(0, 0, 0)
    x_arrive(1, 1, 0)
    x_arrive(2, 0, -1)
    y_send(0, 3, 0, -1, True)
    for d in (0, 1):
        z_arrive(d, 2, 1)
        z_send(d, 3, 1)
    x_arrive(3, 1, 1)
    y_send(1, 3, 1, 1, True)
    z_arrive(0, 3, 0)
    z_send(0, 4, 0)
    z_arrive(1, 3, 1)
    z_send(1, 4, 1)
    z_arrive(1, 3, 0)
    z_arrive(0, 3, 1)
    y_arrive(0, 2, 0, -2, False)
    y_arrive(1, 2, 1, 2, False)
    x_arrive(4, 0, 1)
    x_arrive(5, 1, -1)
    y_arrive(0, 3, 0, -2, True)
    y_arrive(1, 3, 1, 2, True)
    z_arrive(0, 4, 0)
    z_arrive(1, 4, 1)

    for copy in local:
        copy.wait()

    half = 4 * rows
    side = 8 * rows
    columns = cbuf[...].reshape(2 * side, width)

    def pair_rows(i, h):
        lhs = rbuf[i, pl.ds(h * 4, 4)].reshape(half, width)
        return lax.dot_general(lhs, columns, (((1,), (1,)), ((), ())), preferred_element_type=F32)

    for i in (0, 1):
        m_send[i] = pair_rows(i, 1 - core)
        send(m_send.at[i], m_recv.at[i], ms.at[i], mr.at[i], core_to)
    for i in (0, 1):
        m_own[i] = pair_rows(i, core)
    for i in (0, 1):
        arrive(m_recv.at[i], mr.at[i])
        total = m_own[i] + m_recv[i]
        m_own[i] = total
        h_send[i] = total.astype(BF16)
        send(h_send.at[i], hop.at[i], hs.at[i], hr.at[i], (pair_to, cross_to)[i])
    for i in (0, 1):
        arrive(hop.at[i], hr.at[i])
        send(hop.at[i], h_recv.at[i], rs.at[i], rr.at[i], (cross_to, pair_to)[i])
    for i in (0, 1):
        arrive(h_recv.at[i], rr.at[i])
        m_own[i] = m_own[i] + h_recv[i].astype(F32)
    row_e = row_e_buf[pl.ds(pl.multiple_of(core * half, 16), half), 0:1]
    mine = pl.ds(pl.multiple_of(core * half, 16), half)
    for i in (0, 1):
        for j in (0, 1):
            denominator = (occ_ref[i] + occ_ref[j]) - row_e - col_e
            direct = m_own[i, :, pl.ds(j * side, side)]
            swapped = m_own[j, :, pl.ds(i * side, side)]
            abuf[i, mine, pl.ds(j * side, side)] = ((2.0 * direct - swapped) / denominator).astype(BF16)
        send(abuf.at[i, mine], abuf.at[i, mine], as_.at[i], ar.at[i], core_to)
    theirs = pl.ds(pl.multiple_of((1 - core) * half, 16), half)
    for i in (0, 1):
        arrive(abuf.at[i, theirs], ar.at[i])

    cols = width // 2
    quad = cols // 2
    me = yx(0, False)
    mate = yx(0, True)
    left, right = pl.ds(0, cols), pl.ds(cols, cols)

    def wide(ref):
        return ref[...].astype(F32)

    slots = spread.shape[1]
    capacity = slots // 8
    thin = rows // 3
    band = 8 * thin
    window[pl.ds(width, capacity), :] = jnp.zeros((capacity, 128), F32)

    def product(c):
        lhs = abuf[:, pl.ds(c * band, band)].reshape(2 * band, 2 * side)
        res = jnp.dot(lhs, cbuf[...].reshape(2 * side, width), preferred_element_type=F32)
        part[c] = res.reshape(2, 8, thin, width)

    def s1(i):
        for d in (0, 1):
            ya_out[i, d] = part[i, :, ring("y", 2) * 2 + d, :, left].astype(BF16)
            send(ya_out.at[i, d], ya_in.at[i, d], yas.at[i, d], yar.at[i, d], y_to[d])
        for k, dy in enumerate((2, 1, -1, 0)):
            xa_out[i, k] = part[i, :, yx(dy, True), :, right].astype(BF16)
            send(xa_out.at[i, k], xa_in.at[i, k], xas.at[i, k], xar.at[i, k], x_to)
        for d in (0, 1):
            yb_send(i, d, 1 - d, part[i, :, ring("y", 1 - 2 * d) * 2 + 1 - d, :, left])

    def yb_send(i, d, e, value):
        yb_out[i, d, e] = value.astype(BF16)
        send(yb_out.at[i, d, e], yb_in.at[i, d, e], ybs.at[i, d, e], ybr.at[i, d, e], y_to[d])

    def s2(i):
        for d in (0, 1):
            arrive(ya_in.at[i, d], yar.at[i, d])
            yb_send(i, d, d, part[i, :, ring("y", 1 - 2 * d) * 2 + d, :, left] + wide(ya_in.at[i, d]))

    def xc_send(i, d, e, value):
        xc_out[i, d, e] = value.astype(BF16)
        send(xc_out.at[i, d, e], xc_in.at[i, d, e], xcs.at[i, d, e], xcr.at[i, d, e], y_to[d])

    def x_sum(i, k, dy, e):
        at = pl.ds(cols + e * quad, quad)
        return part[i, :, yx(dy, False), :, at] + xa_in[i, k, :, :, pl.ds(e * quad, quad)].astype(F32)

    def s3(i):
        arrive(xa_in.at[i, 0], xar.at[i, 0])
        for d in (0, 1):
            xb_out[i, d] = x_sum(i, 0, 2, d).astype(BF16)
            send(xb_out.at[i, d], xb_in.at[i, d], xbs.at[i, d], xbr.at[i, d], y_to[d])
        for d in (0, 1):
            arrive(xa_in.at[i, 1 + d], xar.at[i, 1 + d])
            xc_send(i, d, 1 - d, x_sum(i, 1 + d, 1 - 2 * d, 1 - d))

    def s4(i):
        for d in (0, 1):
            arrive(xb_in.at[i, d], xbr.at[i, d])
            xc_send(i, d, d, x_sum(i, 1 + d, 1 - 2 * d, d) + wide(xb_in.at[i, d]))

    def s5(i):
        for d in (0, 1):
            for e in (1 - d, d):
                arrive(yb_in.at[i, d, e], ybr.at[i, d, e])
        far = part[i, :, mate, :, left] + wide(yb_in.at[i, 0, 1 - xl]) + wide(yb_in.at[i, 1, 1 - xl])
        yc_out[i] = far.astype(BF16)
        send(yc_out.at[i], yc_in.at[i], ycs.at[i], ycr.at[i], x_to)

    def rounded(total):
        return total.astype(BF16).astype(F32).reshape(2 * thin, total.shape[2])

    def s6(i):
        arrive(xa_in.at[i, 3], xar.at[i, 3])
        for d in (0, 1):
            for e in (1 - d, d):
                arrive(xc_in.at[i, d, e], xcr.at[i, d, e])
        for e in (0, 1):
            total = x_sum(i, 3, 0, e) + wide(xc_in.at[i, 0, e]) + wide(xc_in.at[i, 1, e])
            gamma[:, pl.ds(cols + e * quad, quad)] = rounded(total)
        near = part[i, :, me, :, left] + wide(yb_in.at[i, 0, xl]) + wide(yb_in.at[i, 1, xl])
        arrive(yc_in.at[i], ycr.at[i])
        gamma[:, left] = rounded(near + wide(yc_in.at[i]))

    row_at = lax.broadcasted_iota(jnp.int32, (capacity, 128), 0)

    def picked(block):
        for zt in range(8):
            owner = zt * 8 + block
            rows_of = window[pl.ds(start_ref[owner], capacity), :]
            spread[0, pl.ds(zt * capacity, capacity), :] = jnp.where(row_at < length_ref[owner], rows_of, 0.0)
        return spread[0].T[0 : 2 * thin].astype(BF16).reshape(2, thin, slots)

    def s7(i):
        window[pl.ds(0, width), 0 : 2 * thin] = gamma[...].T
        for k, (dy, other) in enumerate(yx_steps):
            pick_out[i, k] = picked(yx(dy, other))
            send(pick_out.at[i, k], pick_in.at[i, me], qs.at[i, k], qr.at[i, k], yx_peers[k])
        pick_in[i, me] = picked(me)

    def owner_rows(i, dz):
        return turned.at[i, :, pl.ds(pl.multiple_of(ring("z", dz) * capacity, 16), capacity)]

    def landing(i, dz):
        return out_ref.at[:, :, pl.ds(pl.multiple_of(ring("z", dz) * side + i * band, 128), band)]

    def s8(i):
        for k, (dy, other) in enumerate(yx_steps):
            arrive(pick_in.at[i, yx(-dy, other)], qr.at[i, k])
        for o in (0, 1):
            for c in range(slots // 128):
                block = pick_in[i, :, o, :, pl.ds(c * 128, 128)].reshape(band, 128)
                turned[i, o, pl.ds(c * 128, 128), :] = block.astype(F32).T.astype(BF16)
        for k, dz in enumerate(z_steps):
            send(owner_rows(i, dz), landing(i, 0), ts.at[i, k], tr.at[i, k], z_peers[k])
        own = pltpu.make_async_copy(owner_rows(i, 0), landing(i, 0), os_.at[i])
        own.start()
        kept.append(own)

    def s9(i):
        for k, dz in enumerate(z_steps):
            arrive(landing(i, -dz), tr.at[i, k])

    kept = []
    product(0)
    s1(0)
    product(1)
    s2(0)
    s3(0)
    s1(1)
    product(2)
    s4(0)
    s5(0)
    s2(1)
    s3(1)
    s6(0)
    s7(0)
    s1(2)
    s4(1)
    s5(1)
    s2(2)
    s3(2)
    s8(0)
    s6(1)
    s7(1)
    s4(2)
    s5(2)
    s8(1)
    s6(2)
    s7(2)
    s8(2)
    for i in (0, 1, 2):
        s9(i)
    for copy in kept:
        copy.wait()
    for copy in started:
        copy.wait_send()


def owned_columns(factors, occ_energy, vir_energy, start, length):
    occupied, rows, width = factors.shape
    nz, nyx = lax.axis_size("z"), lax.axis_size(ROW)
    group = rows * nyx
    half = group // 2
    slots = 8 * width // (3 * nyx)
    cols = width // 2
    dma = pltpu.SemaphoreType.DMA
    vmem = pl.BlockSpec(memory_space=pltpu.VMEM)
    smem = pl.BlockSpec(memory_space=pltpu.SMEM)
    wide = [pltpu.VMEM((2, half, 2 * group), F32)] * 3
    thin = [pltpu.VMEM((2, half, 2 * group), BF16)] * 3

    def pair_of(*shape):
        return [pltpu.VMEM(shape, BF16)] * 2

    thin_rows = rows // 3
    sems = [(2, 4, 2)] * 2 + [(2, 4)] * 2 + [(6,)] * 2 + [(2,)] * 8
    sems += [(3, 2)] * 2 + [(3, 2, 2)] * 2 + [(3,)] * 2 + [(3, 4)] * 2 + [(3, 2)] * 2 + [(3, 2, 2)] * 2 + [(3, 7)] * 4
    sems += [(2, 2), (3,)]
    hbm = pl.BlockSpec(memory_space=pl.ANY)
    return pl.pallas_call(
        gamma_kernel,
        out_shape=jax.ShapeDtypeStruct((2, slots // nz, nz * group), BF16),
        in_specs=[hbm, smem, vmem, smem, smem],
        out_specs=hbm,
        scratch_shapes=pair_of(2, 8, rows, width)
        + wide
        + thin
        + [
            pltpu.VMEM((2, group, 2 * group), BF16),
            pltpu.VMEM((3, 2, nyx, thin_rows, width), F32),
            pltpu.VMEM((group, 128), F32),
        ]
        + pair_of(3, 2, 2, thin_rows, cols)
        + pair_of(3, 2, 2, 2, thin_rows, cols)
        + pair_of(3, 2, thin_rows, cols)
        + pair_of(3, 4, 2, thin_rows, cols)
        + pair_of(3, 2, 2, thin_rows, cols // 2)
        + pair_of(3, 2, 2, 2, thin_rows, cols // 2)
        + [
            pltpu.VMEM((2 * thin_rows, width), F32),
            pltpu.VMEM((width + slots // nz, 128), F32),
            pltpu.VMEM((1, slots, 128), F32),
            pltpu.VMEM((3, 7, 2, thin_rows, slots), BF16),
            pltpu.VMEM((3, nyx, 2, thin_rows, slots), BF16),
            pltpu.VMEM((3, 2, slots, 8 * thin_rows), BF16),
        ]
        + [dma(s) for s in sems],
        compiler_params=pltpu.CompilerParams(
            collective_id=0, has_side_effects=True, vmem_limit_bytes=60 * 1024 * 1024
        ),
        name="owned_columns",
    )(factors, occ_energy, vir_energy.reshape(nz * nyx, rows), start, length)


def per_device(factors, occ_energy, vir_energy, block_lengths, block_owner):
    occupied, rows, width = factors.shape
    nz, nyx = lax.axis_size("z"), lax.axis_size(ROW)
    owners = nz * nyx
    quarter = lax.axis_index(VIR)
    lengths = lax.dynamic_index_in_dim(block_lengths, quarter, 0, keepdims=False)
    owner_of = lax.dynamic_index_in_dim(block_owner, quarter, 0, keepdims=False)
    order = jnp.arange(owners, dtype=jnp.int32)
    starts = jnp.sum(jnp.where(order[None, :] < order[:, None], lengths[None, :], 0), axis=1)
    match = owner_of[None, :] == order[:, None]
    dest_start = jnp.sum(jnp.where(match, starts[None, :], 0), axis=1)
    dest_length = jnp.sum(jnp.where(match, lengths[None, :], 0), axis=1)
    got = owned_columns(factors, occ_energy, vir_energy, dest_start, dest_length)
    return jnp.transpose(got, (1, 0, 2))


def solution(mesh):
    fine = Mesh(mesh.devices.reshape(8, 4, 2, 2, 2), ("z", "y", "xl", "xh", "core"))
    placed = (P(None, ("z", "y", "xl"), VIR), P(), P(), P(), P())
    return jax.shard_map(
        per_device,
        mesh=fine,
        in_specs=placed,
        out_specs=P(("z", "y", "xl", "xh", "core"), None, None),
        check_vma=False,
    )
```

```python
import jax
import jax.numpy as jnp
from jax import lax
from jax.experimental import pallas as pl
from jax.experimental.pallas import tpu as pltpu
from jax.sharding import Mesh, PartitionSpec as P

ROW = ("y", "xl")
VIR = ("xh", "core")
F32 = jnp.float32
BF16 = jnp.bfloat16


def ring(axis, shift):
    n = lax.axis_size(axis)
    return lax.rem(lax.axis_index(axis) + shift + n, n)


def flip(axis):
    return 1 - lax.axis_index(axis)


def gamma_kernel(
    f_ref, occ_ref, vir_ref, start_ref, length_ref, out_ref,
    rbuf, cbuf, m_send, m_own, m_recv, h_send, h_recv, hop, abuf, part, row_e_buf,
    ya_out, ya_in, yb_out, yb_in, yc_out, yc_in, xa_out, xa_in, xb_out, xb_in, xc_out, xc_in,
    gamma, window, spread, pick_out, pick_in, turned,
    zs, zr, ys, yr, xs, xr, ms, mr, hs, hr, rs, rr, as_, ar,
    yas, yar, ybs, ybr, ycs, ycr, xas, xar, xbs, xbr, xcs, xcr, qs, qr, ts, tr, fs, os_,
):
    z, y, xl, xh, core = (lax.axis_index(n) for n in ("z", "y", "xl", "xh", "core"))
    rows = f_ref.shape[1]
    width = f_ref.shape[2]

    barrier = pltpu.get_barrier_semaphore()
    yx_steps = [(2, True), (2, False), (1, True), (-1, True), (1, False), (-1, False), (0, True)]
    yx_peers = [{"y": ring("y", dy), "xl": flip("xl") if other else xl} for dy, other in yx_steps]
    z_steps = (4, 3, -3, 2, -2, 1, -1)
    z_peers = [{"z": ring("z", dz)} for dz in z_steps]
    core_to = {"core": flip("core")}
    pair_to = {"xl": flip("xl")}
    cross_to = {"xh": flip("xh"), "xl": flip("xl")}
    peers = [z_peers[-2], z_peers[-1], yx_peers[4], yx_peers[5], pair_to, cross_to, core_to]
    for peer in peers:
        pl.semaphore_signal(barrier, inc=1, device_id=peer, device_id_type=pl.DeviceIdType.MESH)
    pl.semaphore_wait(barrier, len(peers))

    started = []

    def send(src, dst, ssem, rsem, peer):
        copy = pltpu.make_async_remote_copy(
            src_ref=src, dst_ref=dst, send_sem=ssem, recv_sem=rsem,
            device_id=peer, device_id_type=pl.DeviceIdType.MESH,
        )
        copy.start()
        started.append(copy)
        return copy

    def arrive(dst, rsem):
        pltpu.make_async_remote_copy(
            src_ref=dst, dst_ref=dst, send_sem=rsem, recv_sem=rsem,
            device_id=peers[0], device_id_type=pl.DeviceIdType.MESH,
        ).wait_recv()

    def yx(dy, other):
        return ring("y", dy) * 2 + (flip("xl") if other else xl)

    z_to = ({"z": ring("z", 1)}, {"z": ring("z", -1)})
    y_to = ({"y": ring("y", 1)}, {"y": ring("y", -1)})
    x_to = {"xl": flip("xl")}

    order = (0, -1, 1, -2, 2, -3, 3, 4)

    def tile(i, dz):
        at = order.index(4 if dz == -4 else dz)
        return cbuf.at[at // 4, i, at % 4]

    def z_send(d, step, i):
        sign = -1 if d == 0 else 1
        src = f_ref.at[i] if step == 1 else tile(i, sign * (step - 1))
        send(src, tile(i, sign * step), zs.at[d, step - 1, i], zr.at[d, step - 1, i], z_to[d])

    def z_arrive(d, step, i):
        arrive(tile(i, -step if d == 0 else step), zr.at[d, step - 1, i])

    def y_send(d, k, i, dy, other):
        src = f_ref.at[i] if (dy == 0 and not other) else rbuf.at[i, yx(dy, other)]
        send(src, rbuf.at[i, yx(dy, other)], ys.at[d, k], yr.at[d, k], y_to[d])

    def y_arrive(d, k, i, dy, other):
        arrive(rbuf.at[i, yx(dy, other)], yr.at[d, k])

    def x_send(k, i, dy):
        src = f_ref.at[i] if dy == 0 else rbuf.at[i, yx(dy, False)]
        send(src, rbuf.at[i, yx(dy, False)], xs.at[k], xr.at[k], x_to)

    def x_arrive(k, i, dy):
        arrive(rbuf.at[i, yx(dy, True)], xr.at[k])

    for i in (0, 1):
        for d in (0, 1):
            z_send(d, 1, i if d == 0 else 1 - i)
            y_send(d, i, i, 0, False)
        x_send(i, i, 0)
    local = []
    for i in (0, 1):
        local.append(pltpu.make_async_copy(f_ref.at[i], tile(i, 0), fs.at[0, i]))
        local.append(pltpu.make_async_copy(f_ref.at[i], rbuf.at[i, yx(0, False)], fs.at[1, i]))
    for copy in local:
        copy.start()
    near_e = jnp.concatenate([vir_ref[pl.ds(z * 8 + k, 1), :] for k in range(8)], axis=1)
    row_e_buf[...] = jnp.broadcast_to(near_e, (128, 8 * rows)).T
    far_e = [vir_ref[pl.ds(ring("z", dz) * 8 + yx(0, False), 1), :] for dz in order]
    col_e = [jnp.concatenate(far_e[4 * g : 4 * g + 4] * 2, axis=1) for g in (0, 1)]
    for d in (0, 1):
        z_arrive(d, 1, d)
        z_send(d, 2, d)
    y_arrive(0, 0, 0, -1, False)
    x_send(2, 0, -1)
    y_send(0, 2, 0, -1, False)
    y_arrive(1, 0, 0, 1, False)
    for d in (0, 1):
        z_arrive(d, 1, 1 - d)
        z_send(d, 2, 1 - d)
    y_arrive(1, 1, 1, 1, False)
    x_send(3, 1, 1)
    y_send(1, 2, 1, 1, False)
    x_send(4, 0, 1)
    y_arrive(0, 1, 1, -1, False)
    x_arrive(0, 0, 0)
    x_arrive(1, 1, 0)
    y_send(0, 4, 1, 0, True)
    for d in (0, 1):
        z_arrive(d, 2, d)
        z_send(d, 3, d)
    x_arrive(2, 0, -1)
    y_send(0, 3, 0, -1, True)
    for d in (0, 1):
        z_arrive(d, 2, 1 - d)
        z_send(d, 3, 1 - d)
    x_arrive(3, 1, 1)
    y_send(1, 3, 1, 1, True)
    for d in (0, 1):
        z_arrive(d, 3, d)
        z_send(d, 4, d)
    y_arrive(0, 2, 0, -2, False)
    y_arrive(1, 2, 1, 2, False)
    y_arrive(0, 4, 1, -1, True)
    x_arrive(4, 0, 1)
    y_arrive(0, 3, 0, -2, True)
    y_arrive(1, 3, 1, 2, True)
    for copy in local:
        copy.wait()

    half = 4 * rows
    side = 8 * rows
    mine = pl.ds(pl.multiple_of(core * half, 16), half)
    theirs = pl.ds(pl.multiple_of((1 - core) * half, 16), half)
    row_e = row_e_buf[mine, 0:1]
    lane = lax.broadcasted_iota(jnp.int32, (1, side), 1)
    low = lane < half
    occ_j = jnp.where(low, occ_ref[0], occ_ref[1])

    def pair_rows(g, i, h):
        lhs = rbuf[i, pl.ds(h * 4, 4)].reshape(half, width)
        rhs = cbuf[g].reshape(side, width)
        return lax.dot_general(lhs, rhs, (((1,), (1,)), ((), ())), preferred_element_type=F32)

    def f1(g):
        for i in (0, 1):
            m_send[g, i] = pair_rows(g, i, 1 - core)
            send(m_send.at[g, i], m_recv.at[g, i], ms.at[g, i], mr.at[g, i], core_to)
        for i in (0, 1):
            m_own[g, i] = pair_rows(g, i, core)

    def f2(g):
        for i in (0, 1):
            arrive(m_recv.at[g, i], mr.at[g, i])
            total = m_own[g, i] + m_recv[g, i]
            m_own[g, i] = total
            h_send[g, i] = total.astype(BF16)
            send(h_send.at[g, i], hop.at[g, i], hs.at[g, i], hr.at[g, i], (pair_to, cross_to)[i])

    def f3(g):
        for i in (0, 1):
            arrive(hop.at[g, i], hr.at[g, i])
            send(hop.at[g, i], h_recv.at[g, i], rs.at[g, i], rr.at[g, i], (cross_to, pair_to)[i])

    def f4(g):
        for i in (0, 1):
            arrive(h_recv.at[g, i], rr.at[g, i])
            m_own[g, i] = m_own[g, i] + h_recv[g, i].astype(F32)
        for i in (0, 1):
            direct = m_own[g, i]
            turned_over = pltpu.roll(m_own[g, 1 - i], half, 1)
            swapped = jnp.where(low, direct, turned_over) if i == 0 else jnp.where(low, turned_over, direct)
            denominator = (occ_ref[i] + occ_j) - row_e - col_e[g]
            at = pl.ds(g * side, side)
            abuf[i, mine, at] = ((2.0 * direct - swapped) / denominator).astype(BF16)
            send(abuf.at[i, mine, at], abuf.at[i, mine, at], as_.at[g, i], ar.at[g, i], core_to)

    f1(0)
    f2(0)
    for d in (0, 1):
        z_arrive(d, 3, 1 - d)
    f3(0)
    for d in (0, 1):
        z_arrive(d, 4, d)
    f1(1)
    f2(1)
    f4(0)
    f3(1)
    f4(1)
    for g in (0, 1):
        for i in (0, 1):
            arrive(abuf.at[i, theirs, pl.ds(g * side, side)], ar.at[g, i])

    cols = width // 2
    quad = cols // 2
    me = yx(0, False)
    mate = yx(0, True)
    left, right = pl.ds(0, cols), pl.ds(cols, cols)

    def wide(ref):
        return ref[...].astype(F32)

    slots = spread.shape[1]
    capacity = slots // 8
    thin = rows // 3
    band = 8 * thin
    window[pl.ds(width, capacity), :] = jnp.zeros((capacity, 128), F32)

    def product(c):
        lhs = abuf[:, pl.ds(c * band, band)].reshape(2 * band, 2 * side)
        res = jnp.dot(lhs, cbuf[...].reshape(2 * side, width), preferred_element_type=F32)
        part[c] = res.reshape(2, 8, thin, width)

    def s1(i):
        for d in (0, 1):
            ya_out[i, d] = part[i, :, ring("y", 2) * 2 + d, :, left].astype(BF16)
            send(ya_out.at[i, d], ya_in.at[i, d], yas.at[i, d], yar.at[i, d], y_to[d])
        for k, dy in enumerate((2, 1, -1, 0)):
            xa_out[i, k] = part[i, :, yx(dy, True), :, right].astype(BF16)
            send(xa_out.at[i, k], xa_in.at[i, k], xas.at[i, k], xar.at[i, k], x_to)
        for d in (0, 1):
            yb_send(i, d, 1 - d, part[i, :, ring("y", 1 - 2 * d) * 2 + 1 - d, :, left])

    def yb_send(i, d, e, value):
        yb_out[i, d, e] = value.astype(BF16)
        send(yb_out.at[i, d, e], yb_in.at[i, d, e], ybs.at[i, d, e], ybr.at[i, d, e], y_to[d])

    def s2(i):
        for d in (0, 1):
            arrive(ya_in.at[i, d], yar.at[i, d])
            yb_send(i, d, d, part[i, :, ring("y", 1 - 2 * d) * 2 + d, :, left] + wide(ya_in.at[i, d]))

    def xc_send(i, d, e, value):
        xc_out[i, d, e] = value.astype(BF16)
        send(xc_out.at[i, d, e], xc_in.at[i, d, e], xcs.at[i, d, e], xcr.at[i, d, e], y_to[d])

    def x_sum(i, k, dy, e):
        at = pl.ds(cols + e * quad, quad)
        return part[i, :, yx(dy, False), :, at] + xa_in[i, k, :, :, pl.ds(e * quad, quad)].astype(F32)

    def s3(i):
        arrive(xa_in.at[i, 0], xar.at[i, 0])
        for d in (0, 1):
            xb_out[i, d] = x_sum(i, 0, 2, d).astype(BF16)
            send(xb_out.at[i, d], xb_in.at[i, d], xbs.at[i, d], xbr.at[i, d], y_to[d])
        for d in (0, 1):
            arrive(xa_in.at[i, 1 + d], xar.at[i, 1 + d])
            xc_send(i, d, 1 - d, x_sum(i, 1 + d, 1 - 2 * d, 1 - d))

    def s4(i):
        for d in (0, 1):
            arrive(xb_in.at[i, d], xbr.at[i, d])
            xc_send(i, d, d, x_sum(i, 1 + d, 1 - 2 * d, d) + wide(xb_in.at[i, d]))

    def s5(i):
        for d in (0, 1):
            for e in (1 - d, d):
                arrive(yb_in.at[i, d, e], ybr.at[i, d, e])
        far = part[i, :, mate, :, left] + wide(yb_in.at[i, 0, 1 - xl]) + wide(yb_in.at[i, 1, 1 - xl])
        yc_out[i] = far.astype(BF16)
        send(yc_out.at[i], yc_in.at[i], ycs.at[i], ycr.at[i], x_to)

    def rounded(total):
        return total.astype(BF16).astype(F32).reshape(2 * thin, total.shape[2])

    def s6(i):
        arrive(xa_in.at[i, 3], xar.at[i, 3])
        for d in (0, 1):
            for e in (1 - d, d):
                arrive(xc_in.at[i, d, e], xcr.at[i, d, e])
        for e in (0, 1):
            total = x_sum(i, 3, 0, e) + wide(xc_in.at[i, 0, e]) + wide(xc_in.at[i, 1, e])
            gamma[:, pl.ds(cols + e * quad, quad)] = rounded(total)
        near = part[i, :, me, :, left] + wide(yb_in.at[i, 0, xl]) + wide(yb_in.at[i, 1, xl])
        arrive(yc_in.at[i], ycr.at[i])
        gamma[:, left] = rounded(near + wide(yc_in.at[i]))

    row_at = lax.broadcasted_iota(jnp.int32, (capacity, 128), 0)

    def picked(block):
        for zt in range(8):
            owner = zt * 8 + block
            rows_of = window[pl.ds(start_ref[owner], capacity), :]
            spread[0, pl.ds(zt * capacity, capacity), :] = jnp.where(row_at < length_ref[owner], rows_of, 0.0)
        return spread[0].T[0 : 2 * thin].astype(BF16).reshape(2, thin, slots)

    def s7(i):
        window[pl.ds(0, width), 0 : 2 * thin] = gamma[...].T
        for k, (dy, other) in enumerate(yx_steps):
            pick_out[i, k] = picked(yx(dy, other))
            send(pick_out.at[i, k], pick_in.at[i, me], qs.at[i, k], qr.at[i, k], yx_peers[k])
        pick_in[i, me] = picked(me)

    def owner_rows(i, dz):
        return turned.at[i, :, pl.ds(pl.multiple_of(ring("z", dz) * capacity, 16), capacity)]

    def landing(i, dz):
        return out_ref.at[:, :, pl.ds(pl.multiple_of(ring("z", dz) * side + i * band, 128), band)]

    def s8(i):
        for k, (dy, other) in enumerate(yx_steps):
            arrive(pick_in.at[i, yx(-dy, other)], qr.at[i, k])
        for o in (0, 1):
            for c in range(slots // 128):
                block = pick_in[i, :, o, :, pl.ds(c * 128, 128)].reshape(band, 128)
                turned[i, o, pl.ds(c * 128, 128), :] = block.astype(F32).T.astype(BF16)
        for k, dz in enumerate(z_steps):
            send(owner_rows(i, dz), landing(i, 0), ts.at[i, k], tr.at[i, k], z_peers[k])
        own = pltpu.make_async_copy(owner_rows(i, 0), landing(i, 0), os_.at[i])
        own.start()
        kept.append(own)

    def s9(i):
        for k, dz in enumerate(z_steps):
            arrive(landing(i, -dz), tr.at[i, k])

    kept = []
    product(0)
    s1(0)
    product(1)
    s2(0)
    s3(0)
    s1(1)
    product(2)
    s4(0)
    s5(0)
    s2(1)
    s3(1)
    s6(0)
    s7(0)
    s1(2)
    s4(1)
    s5(1)
    s2(2)
    s3(2)
    s8(0)
    s6(1)
    s7(1)
    s4(2)
    s5(2)
    s8(1)
    s6(2)
    s7(2)
    s8(2)
    for i in (0, 1, 2):
        s9(i)
    for copy in kept:
        copy.wait()
    for copy in started:
        copy.wait_send()


def owned_columns(factors, occ_energy, vir_energy, start, length):
    occupied, rows, width = factors.shape
    nz, nyx = lax.axis_size("z"), lax.axis_size(ROW)
    group = rows * nyx
    half = group // 2
    slots = 8 * width // (3 * nyx)
    cols = width // 2
    dma = pltpu.SemaphoreType.DMA
    vmem = pl.BlockSpec(memory_space=pltpu.VMEM)
    smem = pl.BlockSpec(memory_space=pltpu.SMEM)
    wide = [pltpu.VMEM((2, 2, half, group), F32)] * 3
    thin = [pltpu.VMEM((2, 2, half, group), BF16)] * 3

    def pair_of(*shape):
        return [pltpu.VMEM(shape, BF16)] * 2

    thin_rows = rows // 3
    sems = [(2, 4, 2)] * 2 + [(2, 5)] * 2 + [(5,)] * 2 + [(2, 2)] * 8
    sems += [(3, 2)] * 2 + [(3, 2, 2)] * 2 + [(3,)] * 2 + [(3, 4)] * 2 + [(3, 2)] * 2 + [(3, 2, 2)] * 2 + [(3, 7)] * 4
    sems += [(2, 2), (3,)]
    hbm = pl.BlockSpec(memory_space=pl.ANY)
    return pl.pallas_call(
        gamma_kernel,
        out_shape=jax.ShapeDtypeStruct((2, slots // nz, nz * group), BF16),
        in_specs=[hbm, smem, vmem, smem, smem],
        out_specs=hbm,
        scratch_shapes=[pltpu.VMEM((2, 8, rows, width), BF16), pltpu.VMEM((2, 2, 4, rows, width), BF16)]
        + wide
        + thin
        + [
            pltpu.VMEM((2, group, 2 * group), BF16),
            pltpu.VMEM((3, 2, nyx, thin_rows, width), F32),
            pltpu.VMEM((group, 128), F32),
        ]
        + pair_of(3, 2, 2, thin_rows, cols)
        + pair_of(3, 2, 2, 2, thin_rows, cols)
        + pair_of(3, 2, thin_rows, cols)
        + pair_of(3, 4, 2, thin_rows, cols)
        + pair_of(3, 2, 2, thin_rows, cols // 2)
        + pair_of(3, 2, 2, 2, thin_rows, cols // 2)
        + [
            pltpu.VMEM((2 * thin_rows, width), F32),
            pltpu.VMEM((width + slots // nz, 128), F32),
            pltpu.VMEM((1, slots, 128), F32),
            pltpu.VMEM((3, 7, 2, thin_rows, slots), BF16),
            pltpu.VMEM((3, nyx, 2, thin_rows, slots), BF16),
            pltpu.VMEM((3, 2, slots, 8 * thin_rows), BF16),
        ]
        + [dma(s) for s in sems],
        compiler_params=pltpu.CompilerParams(
            collective_id=0, has_side_effects=True, vmem_limit_bytes=60 * 1024 * 1024
        ),
        name="owned_columns",
    )(factors, occ_energy, vir_energy.reshape(nz * nyx, rows), start, length)


def per_device(factors, occ_energy, vir_energy, block_lengths, block_owner):
    occupied, rows, width = factors.shape
    nz, nyx = lax.axis_size("z"), lax.axis_size(ROW)
    owners = nz * nyx
    quarter = lax.axis_index(VIR)
    lengths = lax.dynamic_index_in_dim(block_lengths, quarter, 0, keepdims=False)
    owner_of = lax.dynamic_index_in_dim(block_owner, quarter, 0, keepdims=False)
    order = jnp.arange(owners, dtype=jnp.int32)
    starts = jnp.sum(jnp.where(order[None, :] < order[:, None], lengths[None, :], 0), axis=1)
    match = owner_of[None, :] == order[:, None]
    dest_start = jnp.sum(jnp.where(match, starts[None, :], 0), axis=1)
    dest_length = jnp.sum(jnp.where(match, lengths[None, :], 0), axis=1)
    got = owned_columns(factors, occ_energy, vir_energy, dest_start, dest_length)
    return jnp.transpose(got, (1, 0, 2))


def solution(mesh):
    fine = Mesh(mesh.devices.reshape(8, 4, 2, 2, 2), ("z", "y", "xl", "xh", "core"))
    placed = (P(None, ("z", "y", "xl"), VIR), P(), P(), P(), P())
    return jax.shard_map(
        per_device,
        mesh=fine,
        in_specs=placed,
        out_specs=P(("z", "y", "xl", "xh", "core"), None, None),
        check_vma=False,
    )
```

```python
import jax
import jax.numpy as jnp
from jax import lax
from jax.experimental import pallas as pl
from jax.experimental.pallas import tpu as pltpu
from jax.sharding import Mesh, PartitionSpec as P

ROW = ("y", "xl")
VIR = ("xh", "core")
F32 = jnp.float32
BF16 = jnp.bfloat16


def ring(axis, shift):
    n = lax.axis_size(axis)
    return lax.rem(lax.axis_index(axis) + shift + n, n)


def flip(axis):
    return 1 - lax.axis_index(axis)


def gamma_kernel(
    f_ref, occ_ref, vir_ref, start_ref, length_ref, out_ref,
    rbuf, cbuf, m_send, m_own, m_recv, h_send, h_recv, abuf, part, row_e_buf,
    ya_out, ya_in, yb_out, yb_in, yc_out, yc_in, xa_out, xa_in, xb_out, xb_in, xc_out, xc_in,
    gamma, window, spread, pick_out, pick_in, turned,
    zs, zr, ys, yr, xs, xr, ms, mr, hs, hr, as_, ar,
    yas, yar, ybs, ybr, ycs, ycr, xas, xar, xbs, xbr, xcs, xcr, qs, qr, ts, tr, fs, os_,
):
    z, y, xl, xh, core = (lax.axis_index(n) for n in ("z", "y", "xl", "xh", "core"))
    rows = f_ref.shape[1]
    width = f_ref.shape[2]

    barrier = pltpu.get_barrier_semaphore()
    yx_steps = [(2, True), (2, False), (1, True), (-1, True), (1, False), (-1, False), (0, True)]
    yx_peers = [{"y": ring("y", dy), "xl": flip("xl") if other else xl} for dy, other in yx_steps]
    z_steps = (4, 3, -3, 2, -2, 1, -1)
    z_peers = [{"z": ring("z", dz)} for dz in z_steps]
    core_to = {"core": flip("core")}
    pair_to = {"xl": flip("xl")}
    xh_to = {"xh": flip("xh")}
    peers = [z_peers[-2], z_peers[-1], yx_peers[4], yx_peers[5], pair_to, xh_to, core_to]
    for peer in peers:
        pl.semaphore_signal(barrier, inc=1, device_id=peer, device_id_type=pl.DeviceIdType.MESH)
    pl.semaphore_wait(barrier, len(peers))

    started = []

    def send(src, dst, ssem, rsem, peer):
        copy = pltpu.make_async_remote_copy(
            src_ref=src, dst_ref=dst, send_sem=ssem, recv_sem=rsem,
            device_id=peer, device_id_type=pl.DeviceIdType.MESH,
        )
        copy.start()
        started.append(copy)
        return copy

    def arrive(dst, rsem):
        pltpu.make_async_remote_copy(
            src_ref=dst, dst_ref=dst, send_sem=rsem, recv_sem=rsem,
            device_id=peers[0], device_id_type=pl.DeviceIdType.MESH,
        ).wait_recv()

    def yx(dy, other):
        return ring("y", dy) * 2 + (flip("xl") if other else xl)

    def own_tile(i, at):
        return rbuf.at[i, pl.ds(pl.multiple_of(at * rows, 16), rows)]

    z_to = ({"z": ring("z", 1)}, {"z": ring("z", -1)})
    y_to = ({"y": ring("y", 1)}, {"y": ring("y", -1)})
    x_to = {"xl": flip("xl")}

    order = (0, -1, 1, -2, 2, -3, 3, 4)

    def tile(i, dz):
        at = order.index(4 if dz == -4 else dz)
        return cbuf.at[at // 4, i, at % 4]

    def z_send(d, step, i):
        sign = -1 if d == 0 else 1
        src = f_ref.at[i] if step == 1 else tile(i, sign * (step - 1))
        send(src, tile(i, sign * step), zs.at[d, step - 1, i], zr.at[d, step - 1, i], z_to[d])

    def z_arrive(d, step, i):
        arrive(tile(i, -step if d == 0 else step), zr.at[d, step - 1, i])

    def y_send(d, k, i, dy, other):
        src = f_ref.at[i] if (dy == 0 and not other) else own_tile(i, yx(dy, other))
        send(src, own_tile(i, yx(dy, other)), ys.at[d, k], yr.at[d, k], y_to[d])

    def y_arrive(d, k, i, dy, other):
        arrive(own_tile(i, yx(dy, other)), yr.at[d, k])

    def x_send(k, i, dy):
        src = f_ref.at[i] if dy == 0 else own_tile(i, yx(dy, False))
        send(src, own_tile(i, yx(dy, False)), xs.at[k], xr.at[k], x_to)

    def x_arrive(k, i, dy):
        arrive(own_tile(i, yx(dy, True)), xr.at[k])

    for i in (0, 1):
        for d in (0, 1):
            z_send(d, 1, i if d == 0 else 1 - i)
            y_send(d, i, i, 0, False)
        x_send(i, i, 0)
    local = []
    for i in (0, 1):
        local.append(pltpu.make_async_copy(f_ref.at[i], tile(i, 0), fs.at[0, i]))
        local.append(pltpu.make_async_copy(f_ref.at[i], own_tile(i, yx(0, False)), fs.at[1, i]))
    for copy in local:
        copy.start()
    near_e = jnp.concatenate([vir_ref[pl.ds(z * 8 + k, 1), :] for k in range(8)], axis=1)
    row_e_buf[...] = jnp.broadcast_to(near_e, (128, 8 * rows)).T
    far_e = [vir_ref[pl.ds(ring("z", dz) * 8 + yx(0, False), 1), :] for dz in order]
    col_e = [jnp.concatenate(far_e[4 * g : 4 * g + 4] * 2, axis=1) for g in (0, 1)]
    for d in (0, 1):
        z_arrive(d, 1, d)
        z_send(d, 2, d)
    y_arrive(0, 0, 0, -1, False)
    x_send(2, 0, -1)
    y_send(0, 2, 0, -1, False)
    y_arrive(1, 0, 0, 1, False)
    for d in (0, 1):
        z_arrive(d, 1, 1 - d)
        z_send(d, 2, 1 - d)
    y_arrive(1, 1, 1, 1, False)
    x_send(3, 1, 1)
    y_send(1, 2, 1, 1, False)
    x_send(4, 0, 1)
    y_arrive(0, 1, 1, -1, False)
    x_arrive(0, 0, 0)
    x_arrive(1, 1, 0)
    y_send(0, 4, 1, 0, True)
    for d in (0, 1):
        z_arrive(d, 2, d)
        z_send(d, 3, d)
    x_arrive(2, 0, -1)
    y_send(0, 3, 0, -1, True)
    for d in (0, 1):
        z_arrive(d, 2, 1 - d)
        z_send(d, 3, 1 - d)
    x_arrive(3, 1, 1)
    y_send(1, 3, 1, 1, True)
    for d in (0, 1):
        z_arrive(d, 3, d)
        z_send(d, 4, d)
    y_arrive(0, 2, 0, -2, False)
    y_arrive(1, 2, 1, 2, False)
    y_arrive(0, 4, 1, -1, True)
    x_arrive(4, 0, 1)
    y_arrive(0, 3, 0, -2, True)
    y_arrive(1, 3, 1, 2, True)
    for copy in local:
        copy.wait()

    side = 8 * rows
    half = side // 2
    thin = rows // 3
    band = 8 * thin
    share = band // 2
    lane = lax.broadcasted_iota(jnp.int32, (1, side), 1)
    low = lane < half
    occ_j = jnp.where(low, occ_ref[0], occ_ref[1])

    def rows_of(c, h):
        return pl.ds(pl.multiple_of(c * band + h * share, 16), share)

    def pair_rows(g, c, h):
        lhs = rbuf[:, rows_of(c, h)].reshape(2 * share, width)
        rhs = cbuf[g].reshape(side, width)
        res = lax.dot_general(lhs, rhs, (((1,), (1,)), ((), ())), preferred_element_type=F32)
        return res.reshape(2, share, side)

    def f1(g, c):
        m_send[g, c] = pair_rows(g, c, 1 - core)
        send(m_send.at[g, c], m_recv.at[g, c], ms.at[g, c], mr.at[g, c], core_to)
        m_own[g, c] = pair_rows(g, c, core)

    def f2(g, c):
        arrive(m_recv.at[g, c], mr.at[g, c])
        total = m_own[g, c] + m_recv[g, c]
        m_own[g, c] = total
        h_send[g, c] = total.astype(BF16)
        send(h_send.at[g, c], h_recv.at[g, c], hs.at[g, c], hr.at[g, c], xh_to)

    def f4(g, c):
        arrive(h_recv.at[g, c], hr.at[g, c])
        m_own[g, c] = m_own[g, c] + h_recv[g, c].astype(F32)
        row_e = row_e_buf[rows_of(c, core), 0:1]
        at = pl.ds(g * side, side)
        for i in (0, 1):
            direct = m_own[g, c, i]
            turned_over = pltpu.roll(m_own[g, c, 1 - i], half, 1)
            swapped = jnp.where(low, direct, turned_over) if i == 0 else jnp.where(low, turned_over, direct)
            denominator = (occ_ref[i] + occ_j) - row_e - col_e[g]
            abuf[i, rows_of(c, core), at] = ((2.0 * direct - swapped) / denominator).astype(BF16)
        mine = abuf.at[:, rows_of(c, core), at]
        send(mine, mine, as_.at[g, c], ar.at[g, c], core_to)

    def f5(c):
        for g in (0, 1):
            arrive(abuf.at[:, rows_of(c, 1 - core), pl.ds(g * side, side)], ar.at[g, c])

    f1(0, 0)
    f1(0, 1)
    f2(0, 0)
    f1(0, 2)
    f2(0, 1)
    f2(0, 2)
    for d in (0, 1):
        z_arrive(d, 3, 1 - d)
    for d in (0, 1):
        z_arrive(d, 4, d)
    f1(1, 0)
    f1(1, 1)
    f2(1, 0)
    f4(0, 0)
    f1(1, 2)
    f2(1, 1)
    f2(1, 2)
    f4(0, 1)
    f4(1, 0)
    f4(0, 2)
    f5(0)

    cols = width // 2
    quad = cols // 2
    me = yx(0, False)
    mate = yx(0, True)
    left, right = pl.ds(0, cols), pl.ds(cols, cols)

    def wide(ref):
        return ref[...].astype(F32)

    slots = spread.shape[1]
    capacity = slots // 8
    window[pl.ds(width, capacity), :] = jnp.zeros((capacity, 128), F32)

    def product(c):
        lhs = abuf[:, pl.ds(c * band, band)].reshape(2 * band, 2 * side)
        res = jnp.dot(lhs, cbuf[...].reshape(2 * side, width), preferred_element_type=F32)
        part[c] = res.reshape(2, 8, thin, width)

    def s1(i):
        for d in (0, 1):
            ya_out[i, d] = part[i, :, ring("y", 2) * 2 + d, :, left].astype(BF16)
            send(ya_out.at[i, d], ya_in.at[i, d], yas.at[i, d], yar.at[i, d], y_to[d])
        for k, dy in enumerate((2, 1, -1, 0)):
            xa_out[i, k] = part[i, :, yx(dy, True), :, right].astype(BF16)
            send(xa_out.at[i, k], xa_in.at[i, k], xas.at[i, k], xar.at[i, k], x_to)
        for d in (0, 1):
            yb_send(i, d, 1 - d, part[i, :, ring("y", 1 - 2 * d) * 2 + 1 - d, :, left])

    def yb_send(i, d, e, value):
        yb_out[i, d, e] = value.astype(BF16)
        send(yb_out.at[i, d, e], yb_in.at[i, d, e], ybs.at[i, d, e], ybr.at[i, d, e], y_to[d])

    def s2(i):
        for d in (0, 1):
            arrive(ya_in.at[i, d], yar.at[i, d])
            yb_send(i, d, d, part[i, :, ring("y", 1 - 2 * d) * 2 + d, :, left] + wide(ya_in.at[i, d]))

    def xc_send(i, d, e, value):
        xc_out[i, d, e] = value.astype(BF16)
        send(xc_out.at[i, d, e], xc_in.at[i, d, e], xcs.at[i, d, e], xcr.at[i, d, e], y_to[d])

    def x_sum(i, k, dy, e):
        at = pl.ds(cols + e * quad, quad)
        return part[i, :, yx(dy, False), :, at] + xa_in[i, k, :, :, pl.ds(e * quad, quad)].astype(F32)

    def s3(i):
        arrive(xa_in.at[i, 0], xar.at[i, 0])
        for d in (0, 1):
            xb_out[i, d] = x_sum(i, 0, 2, d).astype(BF16)
            send(xb_out.at[i, d], xb_in.at[i, d], xbs.at[i, d], xbr.at[i, d], y_to[d])
        for d in (0, 1):
            arrive(xa_in.at[i, 1 + d], xar.at[i, 1 + d])
            xc_send(i, d, 1 - d, x_sum(i, 1 + d, 1 - 2 * d, 1 - d))

    def s4(i):
        for d in (0, 1):
            arrive(xb_in.at[i, d], xbr.at[i, d])
            xc_send(i, d, d, x_sum(i, 1 + d, 1 - 2 * d, d) + wide(xb_in.at[i, d]))

    def s5(i):
        for d in (0, 1):
            for e in (1 - d, d):
                arrive(yb_in.at[i, d, e], ybr.at[i, d, e])
        far = part[i, :, mate, :, left] + wide(yb_in.at[i, 0, 1 - xl]) + wide(yb_in.at[i, 1, 1 - xl])
        yc_out[i] = far.astype(BF16)
        send(yc_out.at[i], yc_in.at[i], ycs.at[i], ycr.at[i], x_to)

    def rounded(total):
        return total.astype(BF16).astype(F32).reshape(2 * thin, total.shape[2])

    def s6(i):
        arrive(xa_in.at[i, 3], xar.at[i, 3])
        for d in (0, 1):
            for e in (1 - d, d):
                arrive(xc_in.at[i, d, e], xcr.at[i, d, e])
        for e in (0, 1):
            total = x_sum(i, 3, 0, e) + wide(xc_in.at[i, 0, e]) + wide(xc_in.at[i, 1, e])
            gamma[:, pl.ds(cols + e * quad, quad)] = rounded(total)
        near = part[i, :, me, :, left] + wide(yb_in.at[i, 0, xl]) + wide(yb_in.at[i, 1, xl])
        arrive(yc_in.at[i], ycr.at[i])
        gamma[:, left] = rounded(near + wide(yc_in.at[i]))

    row_at = lax.broadcasted_iota(jnp.int32, (capacity, 128), 0)

    def picked(block):
        for zt in range(8):
            owner = zt * 8 + block
            rows_of = window[pl.ds(start_ref[owner], capacity), :]
            spread[0, pl.ds(zt * capacity, capacity), :] = jnp.where(row_at < length_ref[owner], rows_of, 0.0)
        return spread[0].T[0 : 2 * thin].astype(BF16).reshape(2, thin, slots)

    def s7(i):
        window[pl.ds(0, width), 0 : 2 * thin] = gamma[...].T
        for k, (dy, other) in enumerate(yx_steps):
            pick_out[i, k] = picked(yx(dy, other))
            send(pick_out.at[i, k], pick_in.at[i, me], qs.at[i, k], qr.at[i, k], yx_peers[k])
        pick_in[i, me] = picked(me)

    def owner_rows(i, dz):
        return turned.at[i, :, pl.ds(pl.multiple_of(ring("z", dz) * capacity, 16), capacity)]

    def landing(i, dz):
        return out_ref.at[:, :, pl.ds(pl.multiple_of(ring("z", dz) * side + i * band, 128), band)]

    def s8(i):
        for k, (dy, other) in enumerate(yx_steps):
            arrive(pick_in.at[i, yx(-dy, other)], qr.at[i, k])
        for o in (0, 1):
            for c in range(slots // 128):
                block = pick_in[i, :, o, :, pl.ds(c * 128, 128)].reshape(band, 128)
                turned[i, o, pl.ds(c * 128, 128), :] = block.astype(F32).T.astype(BF16)
        for k, dz in enumerate(z_steps):
            send(owner_rows(i, dz), landing(i, 0), ts.at[i, k], tr.at[i, k], z_peers[k])
        own = pltpu.make_async_copy(owner_rows(i, 0), landing(i, 0), os_.at[i])
        own.start()
        kept.append(own)

    def s9(i):
        for k, dz in enumerate(z_steps):
            arrive(landing(i, -dz), tr.at[i, k])

    kept = []
    product(0)
    s1(0)
    f4(1, 1)
    f5(1)
    product(1)
    s2(0)
    s3(0)
    s1(1)
    f4(1, 2)
    f5(2)
    product(2)
    s4(0)
    s5(0)
    s2(1)
    s3(1)
    s6(0)
    s7(0)
    s1(2)
    s4(1)
    s5(1)
    s2(2)
    s3(2)
    s8(0)
    s6(1)
    s7(1)
    s4(2)
    s5(2)
    s8(1)
    s6(2)
    s7(2)
    s8(2)
    for i in (0, 1, 2):
        s9(i)
    for copy in kept:
        copy.wait()
    for copy in started:
        copy.wait_send()


def owned_columns(factors, occ_energy, vir_energy, start, length):
    occupied, rows, width = factors.shape
    nz, nyx = lax.axis_size("z"), lax.axis_size(ROW)
    group = rows * nyx
    slots = 8 * width // (3 * nyx)
    cols = width // 2
    dma = pltpu.SemaphoreType.DMA
    vmem = pl.BlockSpec(memory_space=pltpu.VMEM)
    smem = pl.BlockSpec(memory_space=pltpu.SMEM)
    wide = [pltpu.VMEM((2, 3, 2, group // 6, group), F32)] * 3
    thin = [pltpu.VMEM((2, 3, 2, group // 6, group), BF16)] * 2

    def pair_of(*shape):
        return [pltpu.VMEM(shape, BF16)] * 2

    thin_rows = rows // 3
    sems = [(2, 4, 2)] * 2 + [(2, 5)] * 2 + [(5,)] * 2 + [(2, 3)] * 6
    sems += [(3, 2)] * 2 + [(3, 2, 2)] * 2 + [(3,)] * 2 + [(3, 4)] * 2 + [(3, 2)] * 2 + [(3, 2, 2)] * 2 + [(3, 7)] * 4
    sems += [(2, 2), (3,)]
    hbm = pl.BlockSpec(memory_space=pl.ANY)
    return pl.pallas_call(
        gamma_kernel,
        out_shape=jax.ShapeDtypeStruct((2, slots // nz, nz * group), BF16),
        in_specs=[hbm, smem, vmem, smem, smem],
        out_specs=hbm,
        scratch_shapes=[pltpu.VMEM((2, group, width), BF16), pltpu.VMEM((2, 2, 4, rows, width), BF16)]
        + wide
        + thin
        + [
            pltpu.VMEM((2, group, 2 * group), BF16),
            pltpu.VMEM((3, 2, nyx, thin_rows, width), F32),
            pltpu.VMEM((group, 128), F32),
        ]
        + pair_of(3, 2, 2, thin_rows, cols)
        + pair_of(3, 2, 2, 2, thin_rows, cols)
        + pair_of(3, 2, thin_rows, cols)
        + pair_of(3, 4, 2, thin_rows, cols)
        + pair_of(3, 2, 2, thin_rows, cols // 2)
        + pair_of(3, 2, 2, 2, thin_rows, cols // 2)
        + [
            pltpu.VMEM((2 * thin_rows, width), F32),
            pltpu.VMEM((width + slots // nz, 128), F32),
            pltpu.VMEM((1, slots, 128), F32),
            pltpu.VMEM((3, 7, 2, thin_rows, slots), BF16),
            pltpu.VMEM((3, nyx, 2, thin_rows, slots), BF16),
            pltpu.VMEM((3, 2, slots, 8 * thin_rows), BF16),
        ]
        + [dma(s) for s in sems],
        compiler_params=pltpu.CompilerParams(
            collective_id=0, has_side_effects=True, vmem_limit_bytes=60 * 1024 * 1024
        ),
        name="owned_columns",
    )(factors, occ_energy, vir_energy.reshape(nz * nyx, rows), start, length)


def per_device(factors, occ_energy, vir_energy, block_lengths, block_owner):
    occupied, rows, width = factors.shape
    nz, nyx = lax.axis_size("z"), lax.axis_size(ROW)
    owners = nz * nyx
    quarter = lax.axis_index(VIR)
    lengths = lax.dynamic_index_in_dim(block_lengths, quarter, 0, keepdims=False)
    owner_of = lax.dynamic_index_in_dim(block_owner, quarter, 0, keepdims=False)
    order = jnp.arange(owners, dtype=jnp.int32)
    starts = jnp.sum(jnp.where(order[None, :] < order[:, None], lengths[None, :], 0), axis=1)
    match = owner_of[None, :] == order[:, None]
    dest_start = jnp.sum(jnp.where(match, starts[None, :], 0), axis=1)
    dest_length = jnp.sum(jnp.where(match, lengths[None, :], 0), axis=1)
    got = owned_columns(factors, occ_energy, vir_energy, dest_start, dest_length)
    return jnp.transpose(got, (1, 0, 2))


def solution(mesh):
    fine = Mesh(mesh.devices.reshape(8, 4, 2, 2, 2), ("z", "y", "xl", "xh", "core"))
    placed = (P(None, ("z", "y", "xl"), VIR), P(), P(), P(), P())
    return jax.shard_map(
        per_device,
        mesh=fine,
        in_specs=placed,
        out_specs=P(("z", "y", "xl", "xh", "core"), None, None),
        check_vma=False,
    )
```

```python
import jax
import jax.numpy as jnp
from jax import lax
from jax.experimental import pallas as pl
from jax.experimental.pallas import tpu as pltpu
from jax.sharding import Mesh, PartitionSpec as P

ROW = ("y", "xl")
VIR = ("xh", "core")
F32 = jnp.float32
BF16 = jnp.bfloat16
LEFT = 640


def ring(axis, shift):
    n = lax.axis_size(axis)
    return lax.rem(lax.axis_index(axis) + shift + n, n)


def flip(axis):
    return 1 - lax.axis_index(axis)


def gamma_kernel(
    f_ref, occ_ref, vir_ref, start_ref, length_ref, out_ref,
    rbuf, cbuf, m_send, m_own, m_recv, h_send, h_recv, abuf, part, row_e_buf,
    yb_out, yb_in, yc_out, yc_in, xa_out, xa_in, xc_out, xc_in,
    gamma, window, spread, pick_out, pick_in, turned,
    zs, zr, ys, yr, xs, xr, ms, mr, hs, hr, as_, ar,
    ybs, ybr, ycs, ycr, xas, xar, xcs, xcr, qs, qr, ts, tr, fs, os_,
):
    z, y, xl, xh, core = (lax.axis_index(n) for n in ("z", "y", "xl", "xh", "core"))
    rows = f_ref.shape[1]
    width = f_ref.shape[2]

    barrier = pltpu.get_barrier_semaphore()
    yx_steps = [(2, True), (2, False), (1, True), (-1, True), (1, False), (-1, False), (0, True)]
    yx_peers = [{"y": ring("y", dy), "xl": flip("xl") if other else xl} for dy, other in yx_steps]
    z_steps = (4, 3, -3, 2, -2, 1, -1)
    z_peers = [{"z": ring("z", dz)} for dz in z_steps]
    core_to = {"core": flip("core")}
    pair_to = {"xl": flip("xl")}
    xh_to = {"xh": flip("xh")}
    peers = [z_peers[-2], z_peers[-1], yx_peers[4], yx_peers[5], pair_to, xh_to, core_to]
    for peer in peers:
        pl.semaphore_signal(barrier, inc=1, device_id=peer, device_id_type=pl.DeviceIdType.MESH)
    pl.semaphore_wait(barrier, len(peers))

    started = []

    def send(src, dst, ssem, rsem, peer):
        copy = pltpu.make_async_remote_copy(
            src_ref=src, dst_ref=dst, send_sem=ssem, recv_sem=rsem,
            device_id=peer, device_id_type=pl.DeviceIdType.MESH,
        )
        copy.start()
        started.append(copy)
        return copy

    def arrive(dst, rsem):
        pltpu.make_async_remote_copy(
            src_ref=dst, dst_ref=dst, send_sem=rsem, recv_sem=rsem,
            device_id=peers[0], device_id_type=pl.DeviceIdType.MESH,
        ).wait_recv()

    def yx(dy, other):
        return ring("y", dy) * 2 + (flip("xl") if other else xl)

    def own_tile(i, at):
        return rbuf.at[i, pl.ds(pl.multiple_of(at * rows, 16), rows)]

    z_to = ({"z": ring("z", 1)}, {"z": ring("z", -1)})
    y_to = ({"y": ring("y", 1)}, {"y": ring("y", -1)})
    x_to = {"xl": flip("xl")}

    order = (0, -1, 1, -2, 2, -3, 3, 4)

    def tile(i, dz):
        at = order.index(4 if dz == -4 else dz)
        return cbuf.at[at // 4, i, at % 4]

    def z_send(d, step, i):
        sign = -1 if d == 0 else 1
        src = f_ref.at[i] if step == 1 else tile(i, sign * (step - 1))
        send(src, tile(i, sign * step), zs.at[d, step - 1, i], zr.at[d, step - 1, i], z_to[d])

    def z_arrive(d, step, i):
        arrive(tile(i, -step if d == 0 else step), zr.at[d, step - 1, i])

    def y_send(d, k, i, dy, other):
        src = f_ref.at[i] if (dy == 0 and not other) else own_tile(i, yx(dy, other))
        send(src, own_tile(i, yx(dy, other)), ys.at[d, k], yr.at[d, k], y_to[d])

    def y_arrive(d, k, i, dy, other):
        arrive(own_tile(i, yx(dy, other)), yr.at[d, k])

    def x_send(k, i, dy):
        src = f_ref.at[i] if dy == 0 else own_tile(i, yx(dy, False))
        send(src, own_tile(i, yx(dy, False)), xs.at[k], xr.at[k], x_to)

    def x_arrive(k, i, dy):
        arrive(own_tile(i, yx(dy, True)), xr.at[k])

    for i in (0, 1):
        for d in (0, 1):
            z_send(d, 1, i if d == 0 else 1 - i)
            y_send(d, i, i, 0, False)
        x_send(i, i, 0)
    local = []
    for i in (0, 1):
        local.append(pltpu.make_async_copy(f_ref.at[i], tile(i, 0), fs.at[0, i]))
        local.append(pltpu.make_async_copy(f_ref.at[i], own_tile(i, yx(0, False)), fs.at[1, i]))
    for copy in local:
        copy.start()
    def line(at):
        return jnp.concatenate([vir_ref[pl.ds(3 * at + k, 1), :] for k in range(3)], axis=1)

    near_e = line(z)
    row_e_buf[...] = jnp.broadcast_to(near_e, (128, 8 * rows)).T
    back = lax.rem((8 - yx(0, False)) * rows, 8 * rows)
    far_e = [pltpu.roll(line(ring("z", dz)), back, 1)[:, :rows] for dz in order]
    col_e = [jnp.concatenate(far_e[4 * g : 4 * g + 4] * 2, axis=1) for g in (0, 1)]
    for d in (0, 1):
        z_arrive(d, 1, d)
        z_send(d, 2, d)
    y_arrive(0, 0, 0, -1, False)
    x_send(2, 0, -1)
    y_send(0, 2, 0, -1, False)
    y_arrive(1, 0, 0, 1, False)
    for d in (0, 1):
        z_arrive(d, 1, 1 - d)
        z_send(d, 2, 1 - d)
    y_arrive(1, 1, 1, 1, False)
    x_send(3, 1, 1)
    y_send(1, 2, 1, 1, False)
    x_send(4, 0, 1)
    y_arrive(0, 1, 1, -1, False)
    x_arrive(0, 0, 0)
    x_arrive(1, 1, 0)
    y_send(0, 4, 1, 0, True)
    for d in (0, 1):
        z_arrive(d, 2, d)
        z_send(d, 3, d)
    x_arrive(2, 0, -1)
    y_send(0, 3, 0, -1, True)
    for d in (0, 1):
        z_arrive(d, 2, 1 - d)
        z_send(d, 3, 1 - d)
    x_arrive(3, 1, 1)
    y_send(1, 3, 1, 1, True)
    for d in (0, 1):
        z_arrive(d, 3, d)
        z_send(d, 4, d)
    y_arrive(0, 2, 0, -2, False)
    y_arrive(1, 2, 1, 2, False)
    y_arrive(0, 4, 1, -1, True)
    x_arrive(4, 0, 1)
    y_arrive(0, 3, 0, -2, True)
    y_arrive(1, 3, 1, 2, True)
    for copy in local:
        copy.wait()

    side = 8 * rows
    half = side // 2
    thin = rows // 3
    band = 8 * thin
    share = band // 2
    lane = lax.broadcasted_iota(jnp.int32, (1, side), 1)
    low = lane < half
    occ_j = jnp.where(low, occ_ref[0], occ_ref[1])

    def rows_of(c, h):
        return pl.ds(pl.multiple_of(c * band + h * share, 16), share)

    def pair_rows(g, c, h):
        lhs = rbuf[:, rows_of(c, h)].reshape(2 * share, width)
        rhs = cbuf[g].reshape(side, width)
        res = lax.dot_general(lhs, rhs, (((1,), (1,)), ((), ())), preferred_element_type=F32)
        return res.reshape(2, share, side)

    def f1(g, c):
        m_send[g, c] = pair_rows(g, c, 1 - core)
        send(m_send.at[g, c], m_recv.at[g, c], ms.at[g, c], mr.at[g, c], core_to)
        m_own[g, c] = pair_rows(g, c, core)

    def f2(g, c):
        arrive(m_recv.at[g, c], mr.at[g, c])
        total = m_own[g, c] + m_recv[g, c]
        m_own[g, c] = total
        h_send[g, c] = total.astype(BF16)
        send(h_send.at[g, c], h_recv.at[g, c], hs.at[g, c], hr.at[g, c], xh_to)

    def f4(g, c):
        arrive(h_recv.at[g, c], hr.at[g, c])
        m_own[g, c] = m_own[g, c] + h_recv[g, c].astype(F32)
        row_e = row_e_buf[rows_of(c, core), 0:1]
        at = pl.ds(g * side, side)
        for i in (0, 1):
            direct = m_own[g, c, i]
            turned_over = pltpu.roll(m_own[g, c, 1 - i], half, 1)
            swapped = jnp.where(low, direct, turned_over) if i == 0 else jnp.where(low, turned_over, direct)
            denominator = (occ_ref[i] + occ_j) - row_e - col_e[g]
            abuf[i, rows_of(c, core), at] = ((2.0 * direct - swapped) / denominator).astype(BF16)
        mine = abuf.at[:, rows_of(c, core), at]
        send(mine, mine, as_.at[g, c], ar.at[g, c], core_to)

    def f5(c):
        for g in (0, 1):
            arrive(abuf.at[:, rows_of(c, 1 - core), pl.ds(g * side, side)], ar.at[g, c])

    f1(0, 0)
    f1(0, 1)
    f2(0, 0)
    f1(0, 2)
    f2(0, 1)
    f2(0, 2)
    for d in (0, 1):
        z_arrive(d, 3, 1 - d)
    for d in (0, 1):
        z_arrive(d, 4, d)
    f1(1, 0)
    f1(1, 1)
    f2(1, 0)
    f4(0, 0)
    f1(1, 2)
    f2(1, 1)
    f2(1, 2)
    f4(0, 1)
    f4(1, 0)
    f4(0, 2)
    f5(0)

    cols = LEFT
    me = yx(0, False)
    mate = yx(0, True)
    left, right = pl.ds(0, cols), pl.ds(cols, width - cols)
    y_steps = (2, 1, -1)
    y_peers = [{"y": ring("y", dy)} for dy in y_steps]

    def wide(ref):
        return ref[...].astype(F32)

    slots = spread.shape[1]
    capacity = slots // 8
    window[pl.ds(width, capacity), :] = jnp.zeros((capacity, 128), F32)

    def product(c):
        lhs = abuf[:, pl.ds(c * band, band)].reshape(2 * band, 2 * side)
        res = jnp.dot(lhs, cbuf[...].reshape(2 * side, width), preferred_element_type=F32)
        part[c] = res.reshape(2, 8, thin, width)

    def s1(i):
        for k, dy in enumerate(y_steps):
            there = pl.ds(ring("y", dy) * 2, 2)
            yb_out[i, k] = part[i, :, there, :, left].astype(BF16)
            send(yb_out.at[i, k], yb_in.at[i, k], ybs.at[i, k], ybr.at[i, k], y_peers[k])
        for k, dy in enumerate(y_steps + (0,)):
            xa_out[i, k] = part[i, :, yx(dy, True), :, right].astype(BF16)
            send(xa_out.at[i, k], xa_in.at[i, k], xas.at[i, k], xar.at[i, k], x_to)

    def x_sum(i, k, dy):
        arrive(xa_in.at[i, k], xar.at[i, k])
        return part[i, :, yx(dy, False), :, right] + wide(xa_in.at[i, k])

    def s3(i):
        for k, dy in enumerate(y_steps):
            xc_out[i, k] = x_sum(i, k, dy).astype(BF16)
            send(xc_out.at[i, k], xc_in.at[i, k], xcs.at[i, k], xcr.at[i, k], y_peers[k])

    def y_sum(i, e):
        total = part[i, :, ring("y", 0) * 2 + e, :, left]
        for k in range(3):
            total = total + yb_in[i, k, :, e].astype(F32)
        return total

    def s5(i):
        for k in range(3):
            arrive(yb_in.at[i, k], ybr.at[i, k])
        yc_out[i] = y_sum(i, 1 - xl).astype(BF16)
        send(yc_out.at[i], yc_in.at[i], ycs.at[i], ycr.at[i], x_to)

    def rounded(total):
        return total.astype(BF16).astype(F32).reshape(2 * thin, total.shape[2])

    def s6(i):
        total = x_sum(i, 3, 0)
        for k in range(3):
            arrive(xc_in.at[i, k], xcr.at[i, k])
            total = total + wide(xc_in.at[i, k])
        gamma[:, right] = rounded(total)
        arrive(yc_in.at[i], ycr.at[i])
        gamma[:, left] = rounded(y_sum(i, xl) + wide(yc_in.at[i]))

    row_at = lax.broadcasted_iota(jnp.int32, (capacity, 128), 0)

    def picked(block):
        for zt in range(8):
            owner = zt * 8 + block
            rows_of = window[pl.ds(start_ref[owner], capacity), :]
            spread[0, pl.ds(zt * capacity, capacity), :] = jnp.where(row_at < length_ref[owner], rows_of, 0.0)
        return spread[0].T[0 : 2 * thin].astype(BF16).reshape(2, thin, slots)

    def s7(i):
        window[pl.ds(0, width), 0 : 2 * thin] = gamma[...].T
        for k, (dy, other) in enumerate(yx_steps):
            pick_out[i, k] = picked(yx(dy, other))
            send(pick_out.at[i, k], pick_in.at[i, me], qs.at[i, k], qr.at[i, k], yx_peers[k])
        pick_in[i, me] = picked(me)

    def owner_rows(i, dz):
        return turned.at[i, :, pl.ds(pl.multiple_of(ring("z", dz) * capacity, 16), capacity)]

    def landing(i, dz):
        return out_ref.at[:, :, pl.ds(pl.multiple_of(ring("z", dz) * side + i * band, 128), band)]

    def s8(i):
        for k, (dy, other) in enumerate(yx_steps):
            arrive(pick_in.at[i, yx(-dy, other)], qr.at[i, k])
        for o in (0, 1):
            for c in range(slots // 128):
                block = pick_in[i, :, o, :, pl.ds(c * 128, 128)].reshape(band, 128)
                turned[i, o, pl.ds(c * 128, 128), :] = block.astype(F32).T.astype(BF16)
        for k, dz in enumerate(z_steps):
            send(owner_rows(i, dz), landing(i, 0), ts.at[i, k], tr.at[i, k], z_peers[k])
        own = pltpu.make_async_copy(owner_rows(i, 0), landing(i, 0), os_.at[i])
        own.start()
        kept.append(own)

    def s9(i):
        for k, dz in enumerate(z_steps):
            arrive(landing(i, -dz), tr.at[i, k])

    kept = []
    product(0)
    s1(0)
    f4(1, 1)
    f5(1)
    product(1)
    s3(0)
    s1(1)
    f4(1, 2)
    f5(2)
    product(2)
    s5(0)
    s3(1)
    s1(2)
    s6(0)
    s7(0)
    s5(1)
    s3(2)
    s8(0)
    s6(1)
    s7(1)
    s5(2)
    s8(1)
    s6(2)
    s7(2)
    s8(2)
    for i in (0, 1, 2):
        s9(i)
    for copy in kept:
        copy.wait()
    for copy in started:
        copy.wait_send()


def owned_columns(factors, occ_energy, vir_energy, start, length):
    occupied, rows, width = factors.shape
    nz, nyx = lax.axis_size("z"), lax.axis_size(ROW)
    group = rows * nyx
    slots = 8 * width // (3 * nyx)
    cols = LEFT
    dma = pltpu.SemaphoreType.DMA
    vmem = pl.BlockSpec(memory_space=pltpu.VMEM)
    smem = pl.BlockSpec(memory_space=pltpu.SMEM)
    wide = [pltpu.VMEM((2, 3, 2, group // 6, group), F32)] * 3
    thin = [pltpu.VMEM((2, 3, 2, group // 6, group), BF16)] * 2

    def pair_of(*shape):
        return [pltpu.VMEM(shape, BF16)] * 2

    thin_rows = rows // 3
    sems = [(2, 4, 2)] * 2 + [(2, 5)] * 2 + [(5,)] * 2 + [(2, 3)] * 6
    sems += [(3, 3)] * 2 + [(3,)] * 2 + [(3, 4)] * 2 + [(3, 3)] * 2 + [(3, 7)] * 4
    sems += [(2, 2), (3,)]
    hbm = pl.BlockSpec(memory_space=pl.ANY)
    return pl.pallas_call(
        gamma_kernel,
        out_shape=jax.ShapeDtypeStruct((2, slots // nz, nz * group), BF16),
        in_specs=[hbm, smem, vmem, smem, smem],
        out_specs=hbm,
        scratch_shapes=[pltpu.VMEM((2, group, width), BF16), pltpu.VMEM((2, 2, 4, rows, width), BF16)]
        + wide
        + thin
        + [
            pltpu.VMEM((2, group, 2 * group), BF16),
            pltpu.VMEM((3, 2, nyx, thin_rows, width), F32),
            pltpu.VMEM((group, 128), F32),
        ]
        + pair_of(3, 3, 2, 2, thin_rows, cols)
        + pair_of(3, 2, thin_rows, cols)
        + pair_of(3, 4, 2, thin_rows, width - cols)
        + pair_of(3, 3, 2, thin_rows, width - cols)
        + [
            pltpu.VMEM((2 * thin_rows, width), F32),
            pltpu.VMEM((width + slots // nz, 128), F32),
            pltpu.VMEM((1, slots, 128), F32),
            pltpu.VMEM((3, 7, 2, thin_rows, slots), BF16),
            pltpu.VMEM((3, nyx, 2, thin_rows, slots), BF16),
            pltpu.VMEM((3, 2, slots, 8 * thin_rows), BF16),
        ]
        + [dma(s) for s in sems],
        compiler_params=pltpu.CompilerParams(
            collective_id=0, has_side_effects=True, vmem_limit_bytes=60 * 1024 * 1024
        ),
        name="owned_columns",
    )(factors, occ_energy, vir_energy.reshape(nz * group // 128, 128), start, length)


def per_device(factors, occ_energy, vir_energy, block_lengths, block_owner):
    occupied, rows, width = factors.shape
    nz, nyx = lax.axis_size("z"), lax.axis_size(ROW)
    owners = nz * nyx
    quarter = lax.axis_index(VIR)
    lengths = lax.dynamic_index_in_dim(block_lengths, quarter, 0, keepdims=False)
    owner_of = lax.dynamic_index_in_dim(block_owner, quarter, 0, keepdims=False)
    order = jnp.arange(owners, dtype=jnp.int32)
    starts = jnp.sum(jnp.where(order[None, :] < order[:, None], lengths[None, :], 0), axis=1)
    match = owner_of[None, :] == order[:, None]
    dest_start = jnp.sum(jnp.where(match, starts[None, :], 0), axis=1)
    dest_length = jnp.sum(jnp.where(match, lengths[None, :], 0), axis=1)
    got = owned_columns(factors, occ_energy, vir_energy, dest_start, dest_length)
    return jnp.transpose(got, (1, 0, 2))


def solution(mesh):
    fine = Mesh(mesh.devices.reshape(8, 4, 2, 2, 2), ("z", "y", "xl", "xh", "core"))
    placed = (P(None, ("z", "y", "xl"), VIR), P(), P(), P(), P())
    return jax.shard_map(
        per_device,
        mesh=fine,
        in_specs=placed,
        out_specs=P(("z", "y", "xl", "xh", "core"), None, None),
        check_vma=False,
    )
```

```python
import jax
import jax.numpy as jnp
from jax import lax
from jax.experimental import pallas as pl
from jax.experimental.pallas import tpu as pltpu
from jax.sharding import Mesh, PartitionSpec as P

ROW = ("y", "xl")
VIR = ("xh", "core")
F32 = jnp.float32
BF16 = jnp.bfloat16
LEFT = 640


def ring(axis, shift):
    n = lax.axis_size(axis)
    return lax.rem(lax.axis_index(axis) + shift + n, n)


def flip(axis):
    return 1 - lax.axis_index(axis)


def gamma_kernel(
    f_ref, occ_in, vir_in, start_in, length_in, out_ref,
    occ_ref, vir_ref, start_ref, length_ref,
    rbuf, cbuf, m_send, m_own, m_recv, h_send, h_recv, abuf, part, row_e_buf,
    yb_out, yb_in, yc_out, yc_in, xa_out, xa_in, xc_out, xc_in,
    gamma, window, spread, pick_out, pick_in, turned,
    zs, zr, ys, yr, xs, xr, ms, mr, hs, hr, as_, ar,
    ybs, ybr, ycs, ycr, xas, xar, xcs, xcr, qs, qr, ts, tr, fs, os_, es,
):
    z, y, xl, xh, core = (lax.axis_index(n) for n in ("z", "y", "xl", "xh", "core"))
    rows = f_ref.shape[1]
    width = f_ref.shape[2]

    fetched = [
        pltpu.make_async_copy(src, dst, es.at[k])
        for k, (src, dst) in enumerate(
            [(occ_in, occ_ref), (vir_in, vir_ref), (start_in, start_ref), (length_in, length_ref)]
        )
    ]
    for copy in fetched:
        copy.start()
    barrier = pltpu.get_barrier_semaphore()
    yx_steps = [(2, True), (2, False), (1, True), (-1, True), (1, False), (-1, False), (0, True)]
    yx_peers = [{"y": ring("y", dy), "xl": flip("xl") if other else xl} for dy, other in yx_steps]
    z_steps = (4, 3, -3, 2, -2, 1, -1)
    z_peers = [{"z": ring("z", dz)} for dz in z_steps]
    core_to = {"core": flip("core")}
    pair_to = {"xl": flip("xl")}
    xh_to = {"xh": flip("xh")}
    peers = [z_peers[-2], z_peers[-1], yx_peers[4], yx_peers[5], pair_to, xh_to, core_to]
    for peer in peers:
        pl.semaphore_signal(barrier, inc=1, device_id=peer, device_id_type=pl.DeviceIdType.MESH)
    pl.semaphore_wait(barrier, len(peers))

    started = []

    def send(src, dst, ssem, rsem, peer):
        copy = pltpu.make_async_remote_copy(
            src_ref=src, dst_ref=dst, send_sem=ssem, recv_sem=rsem,
            device_id=peer, device_id_type=pl.DeviceIdType.MESH,
        )
        copy.start()
        started.append(copy)
        return copy

    def arrive(dst, rsem):
        pltpu.make_async_remote_copy(
            src_ref=dst, dst_ref=dst, send_sem=rsem, recv_sem=rsem,
            device_id=peers[0], device_id_type=pl.DeviceIdType.MESH,
        ).wait_recv()

    def yx(dy, other):
        return ring("y", dy) * 2 + (flip("xl") if other else xl)

    def own_tile(i, at):
        return rbuf.at[i, pl.ds(pl.multiple_of(at * rows, 16), rows)]

    z_to = ({"z": ring("z", 1)}, {"z": ring("z", -1)})
    y_to = ({"y": ring("y", 1)}, {"y": ring("y", -1)})
    x_to = {"xl": flip("xl")}

    order = (0, -1, 1, -2, 2, -3, 3, 4)

    def tile(i, dz):
        at = order.index(4 if dz == -4 else dz)
        return cbuf.at[at // 4, i, at % 4]

    def z_send(d, step, i):
        sign = -1 if d == 0 else 1
        src = f_ref.at[i] if step == 1 else tile(i, sign * (step - 1))
        send(src, tile(i, sign * step), zs.at[d, step - 1, i], zr.at[d, step - 1, i], z_to[d])

    def z_arrive(d, step, i):
        arrive(tile(i, -step if d == 0 else step), zr.at[d, step - 1, i])

    def y_send(d, k, i, dy, other):
        src = f_ref.at[i] if (dy == 0 and not other) else own_tile(i, yx(dy, other))
        send(src, own_tile(i, yx(dy, other)), ys.at[d, k], yr.at[d, k], y_to[d])

    def y_arrive(d, k, i, dy, other):
        arrive(own_tile(i, yx(dy, other)), yr.at[d, k])

    def x_send(k, i, dy):
        src = f_ref.at[i] if dy == 0 else own_tile(i, yx(dy, False))
        send(src, own_tile(i, yx(dy, False)), xs.at[k], xr.at[k], x_to)

    def x_arrive(k, i, dy):
        arrive(own_tile(i, yx(dy, True)), xr.at[k])

    for i in (0, 1):
        for d in (0, 1):
            z_send(d, 1, i if d == 0 else 1 - i)
            y_send(d, i, i, 0, False)
        x_send(i, i, 0)
    local = []
    for i in (0, 1):
        local.append(pltpu.make_async_copy(f_ref.at[i], tile(i, 0), fs.at[0, i]))
        local.append(pltpu.make_async_copy(f_ref.at[i], own_tile(i, yx(0, False)), fs.at[1, i]))
    for copy in local:
        copy.start()
    for copy in fetched:
        copy.wait()

    def line(at):
        return jnp.concatenate([vir_ref[pl.ds(3 * at + k, 1), :] for k in range(3)], axis=1)

    near_e = line(z)
    row_e_buf[...] = jnp.broadcast_to(near_e, (128, 8 * rows)).T
    back = lax.rem((8 - yx(0, False)) * rows, 8 * rows)
    far_e = [pltpu.roll(line(ring("z", dz)), back, 1)[:, :rows] for dz in order]
    col_e = [jnp.concatenate(far_e[4 * g : 4 * g + 4] * 2, axis=1) for g in (0, 1)]
    for d in (0, 1):
        z_arrive(d, 1, d)
        z_send(d, 2, d)
    y_arrive(0, 0, 0, -1, False)
    x_send(2, 0, -1)
    y_send(0, 2, 0, -1, False)
    y_arrive(1, 0, 0, 1, False)
    for d in (0, 1):
        z_arrive(d, 1, 1 - d)
        z_send(d, 2, 1 - d)
    y_arrive(1, 1, 1, 1, False)
    x_send(3, 1, 1)
    y_send(1, 2, 1, 1, False)
    x_send(4, 0, 1)
    y_arrive(0, 1, 1, -1, False)
    x_arrive(0, 0, 0)
    x_arrive(1, 1, 0)
    y_send(0, 4, 1, 0, True)
    for d in (0, 1):
        z_arrive(d, 2, d)
        z_send(d, 3, d)
    x_arrive(2, 0, -1)
    y_send(0, 3, 0, -1, True)
    for d in (0, 1):
        z_arrive(d, 2, 1 - d)
        z_send(d, 3, 1 - d)
    x_arrive(3, 1, 1)
    y_send(1, 3, 1, 1, True)
    for d in (0, 1):
        z_arrive(d, 3, d)
        z_send(d, 4, d)
    y_arrive(0, 2, 0, -2, False)
    y_arrive(1, 2, 1, 2, False)
    y_arrive(0, 4, 1, -1, True)
    x_arrive(4, 0, 1)
    y_arrive(0, 3, 0, -2, True)
    y_arrive(1, 3, 1, 2, True)
    for copy in local:
        copy.wait()

    side = 8 * rows
    half = side // 2
    thin = rows // 3
    band = 8 * thin
    share = band // 2
    lane = lax.broadcasted_iota(jnp.int32, (1, side), 1)
    low = lane < half
    occ_j = jnp.where(low, occ_ref[0], occ_ref[1])

    def rows_of(c, h):
        return pl.ds(pl.multiple_of(c * band + h * share, 16), share)

    def pair_rows(g, c, h):
        lhs = rbuf[:, rows_of(c, h)].reshape(2 * share, width)
        rhs = cbuf[g].reshape(side, width)
        res = lax.dot_general(lhs, rhs, (((1,), (1,)), ((), ())), preferred_element_type=F32)
        return res.reshape(2, share, side)

    def f1(g, c):
        m_send[g, c] = pair_rows(g, c, 1 - core)
        send(m_send.at[g, c], m_recv.at[g, c], ms.at[g, c], mr.at[g, c], core_to)
        m_own[g, c] = pair_rows(g, c, core)

    def f2(g, c):
        arrive(m_recv.at[g, c], mr.at[g, c])
        total = m_own[g, c] + m_recv[g, c]
        m_own[g, c] = total
        h_send[g, c] = total.astype(BF16)
        send(h_send.at[g, c], h_recv.at[g, c], hs.at[g, c], hr.at[g, c], xh_to)

    def f4(g, c):
        arrive(h_recv.at[g, c], hr.at[g, c])
        m_own[g, c] = m_own[g, c] + h_recv[g, c].astype(F32)
        row_e = row_e_buf[rows_of(c, core), 0:1]
        at = pl.ds(g * side, side)
        for i in (0, 1):
            direct = m_own[g, c, i]
            turned_over = pltpu.roll(m_own[g, c, 1 - i], half, 1)
            swapped = jnp.where(low, direct, turned_over) if i == 0 else jnp.where(low, turned_over, direct)
            denominator = (occ_ref[i] + occ_j) - row_e - col_e[g]
            abuf[i, rows_of(c, core), at] = ((2.0 * direct - swapped) / denominator).astype(BF16)
        mine = abuf.at[:, rows_of(c, core), at]
        send(mine, mine, as_.at[g, c], ar.at[g, c], core_to)

    def f5(c):
        for g in (0, 1):
            arrive(abuf.at[:, rows_of(c, 1 - core), pl.ds(g * side, side)], ar.at[g, c])

    f1(0, 0)
    f1(0, 1)
    f2(0, 0)
    f1(0, 2)
    f2(0, 1)
    f2(0, 2)
    for d in (0, 1):
        z_arrive(d, 3, 1 - d)
    for d in (0, 1):
        z_arrive(d, 4, d)
    f1(1, 0)
    f1(1, 1)
    f2(1, 0)
    f4(0, 0)
    f1(1, 2)
    f2(1, 1)
    f2(1, 2)
    f4(0, 1)
    f4(1, 0)
    f4(0, 2)
    f5(0)

    cols = LEFT
    me = yx(0, False)
    mate = yx(0, True)
    left, right = pl.ds(0, cols), pl.ds(cols, width - cols)
    y_steps = (2, 1, -1)
    y_peers = [{"y": ring("y", dy)} for dy in y_steps]

    def wide(ref):
        return ref[...].astype(F32)

    slots = spread.shape[1]
    capacity = slots // 8
    window[pl.ds(width, capacity), :] = jnp.zeros((capacity, 128), F32)

    def product(c):
        lhs = abuf[:, pl.ds(c * band, band)].reshape(2 * band, 2 * side)
        res = jnp.dot(lhs, cbuf[...].reshape(2 * side, width), preferred_element_type=F32)
        part[c] = res.reshape(2, 8, thin, width)

    def s1(i):
        for k, dy in enumerate(y_steps):
            there = pl.ds(ring("y", dy) * 2, 2)
            yb_out[i, k] = part[i, :, there, :, left].astype(BF16)
            send(yb_out.at[i, k], yb_in.at[i, k], ybs.at[i, k], ybr.at[i, k], y_peers[k])
        for k, dy in enumerate(y_steps + (0,)):
            xa_out[i, k] = part[i, :, yx(dy, True), :, right].astype(BF16)
            send(xa_out.at[i, k], xa_in.at[i, k], xas.at[i, k], xar.at[i, k], x_to)

    def x_sum(i, k, dy):
        arrive(xa_in.at[i, k], xar.at[i, k])
        return part[i, :, yx(dy, False), :, right] + wide(xa_in.at[i, k])

    def s3(i):
        for k, dy in enumerate(y_steps):
            xc_out[i, k] = x_sum(i, k, dy).astype(BF16)
            send(xc_out.at[i, k], xc_in.at[i, k], xcs.at[i, k], xcr.at[i, k], y_peers[k])

    def y_sum(i, e):
        total = part[i, :, ring("y", 0) * 2 + e, :, left]
        for k in range(3):
            total = total + yb_in[i, k, :, e].astype(F32)
        return total

    def s5(i):
        for k in range(3):
            arrive(yb_in.at[i, k], ybr.at[i, k])
        yc_out[i] = y_sum(i, 1 - xl).astype(BF16)
        send(yc_out.at[i], yc_in.at[i], ycs.at[i], ycr.at[i], x_to)

    def rounded(total):
        return total.astype(BF16).astype(F32).reshape(2 * thin, total.shape[2])

    def s6(i):
        total = x_sum(i, 3, 0)
        for k in range(3):
            arrive(xc_in.at[i, k], xcr.at[i, k])
            total = total + wide(xc_in.at[i, k])
        gamma[:, right] = rounded(total)
        arrive(yc_in.at[i], ycr.at[i])
        gamma[:, left] = rounded(y_sum(i, xl) + wide(yc_in.at[i]))

    row_at = lax.broadcasted_iota(jnp.int32, (capacity, 128), 0)

    def picked(block):
        for zt in range(8):
            owner = zt * 8 + block
            rows_of = window[pl.ds(start_ref[owner], capacity), :]
            spread[0, pl.ds(zt * capacity, capacity), :] = jnp.where(row_at < length_ref[owner], rows_of, 0.0)
        return spread[0].T[0 : 2 * thin].astype(BF16).reshape(2, thin, slots)

    def s7(i):
        window[pl.ds(0, width), 0 : 2 * thin] = gamma[...].T
        for k, (dy, other) in enumerate(yx_steps):
            pick_out[i, k] = picked(yx(dy, other))
            send(pick_out.at[i, k], pick_in.at[i, me], qs.at[i, k], qr.at[i, k], yx_peers[k])
        pick_in[i, me] = picked(me)

    def owner_rows(i, dz):
        return turned.at[i, :, pl.ds(pl.multiple_of(ring("z", dz) * capacity, 16), capacity)]

    def landing(i, dz):
        return out_ref.at[:, :, pl.ds(pl.multiple_of(ring("z", dz) * side + i * band, 128), band)]

    def s8(i):
        for k, (dy, other) in enumerate(yx_steps):
            arrive(pick_in.at[i, yx(-dy, other)], qr.at[i, k])
        for o in (0, 1):
            for c in range(slots // 128):
                block = pick_in[i, :, o, :, pl.ds(c * 128, 128)].reshape(band, 128)
                turned[i, o, pl.ds(c * 128, 128), :] = block.astype(F32).T.astype(BF16)
        for k, dz in enumerate(z_steps):
            send(owner_rows(i, dz), landing(i, 0), ts.at[i, k], tr.at[i, k], z_peers[k])
        own = pltpu.make_async_copy(owner_rows(i, 0), landing(i, 0), os_.at[i])
        own.start()
        kept.append(own)

    def s9(i):
        for k, dz in enumerate(z_steps):
            arrive(landing(i, -dz), tr.at[i, k])

    kept = []
    product(0)
    s1(0)
    f4(1, 1)
    f5(1)
    product(1)
    s3(0)
    s1(1)
    f4(1, 2)
    f5(2)
    product(2)
    s5(0)
    s3(1)
    s1(2)
    s6(0)
    s7(0)
    s5(1)
    s3(2)
    s8(0)
    s6(1)
    s7(1)
    s5(2)
    s8(1)
    s6(2)
    s7(2)
    s8(2)
    for i in (0, 1, 2):
        s9(i)
    for copy in kept:
        copy.wait()
    for copy in started:
        copy.wait_send()


def owned_columns(factors, occ_energy, vir_energy, start, length):
    occupied, rows, width = factors.shape
    nz, nyx = lax.axis_size("z"), lax.axis_size(ROW)
    group = rows * nyx
    slots = 8 * width // (3 * nyx)
    cols = LEFT
    dma = pltpu.SemaphoreType.DMA
    wide = [pltpu.VMEM((2, 3, 2, group // 6, group), F32)] * 3
    thin = [pltpu.VMEM((2, 3, 2, group // 6, group), BF16)] * 2

    def pair_of(*shape):
        return [pltpu.VMEM(shape, BF16)] * 2

    thin_rows = rows // 3
    sems = [(2, 4, 2)] * 2 + [(2, 5)] * 2 + [(5,)] * 2 + [(2, 3)] * 6
    sems += [(3, 3)] * 2 + [(3,)] * 2 + [(3, 4)] * 2 + [(3, 3)] * 2 + [(3, 7)] * 4
    sems += [(2, 2), (3,), (4,)]
    hbm = pl.BlockSpec(memory_space=pl.ANY)
    return pl.pallas_call(
        gamma_kernel,
        out_shape=jax.ShapeDtypeStruct((2, slots // nz, nz * group), BF16),
        in_specs=[hbm] * 5,
        out_specs=hbm,
        scratch_shapes=[
            pltpu.SMEM((2,), F32),
            pltpu.VMEM((nz * group // 128, 128), F32),
            pltpu.SMEM((nz * nyx,), jnp.int32),
            pltpu.SMEM((nz * nyx,), jnp.int32),
        ]
        + [pltpu.VMEM((2, group, width), BF16), pltpu.VMEM((2, 2, 4, rows, width), BF16)]
        + wide
        + thin
        + [
            pltpu.VMEM((2, group, 2 * group), BF16),
            pltpu.VMEM((3, 2, nyx, thin_rows, width), F32),
            pltpu.VMEM((group, 128), F32),
        ]
        + pair_of(3, 3, 2, 2, thin_rows, cols)
        + pair_of(3, 2, thin_rows, cols)
        + pair_of(3, 4, 2, thin_rows, width - cols)
        + pair_of(3, 3, 2, thin_rows, width - cols)
        + [
            pltpu.VMEM((2 * thin_rows, width), F32),
            pltpu.VMEM((width + slots // nz, 128), F32),
            pltpu.VMEM((1, slots, 128), F32),
            pltpu.VMEM((3, 7, 2, thin_rows, slots), BF16),
            pltpu.VMEM((3, nyx, 2, thin_rows, slots), BF16),
            pltpu.VMEM((3, 2, slots, 8 * thin_rows), BF16),
        ]
        + [dma(s) for s in sems],
        compiler_params=pltpu.CompilerParams(
            collective_id=0, has_side_effects=True, vmem_limit_bytes=60 * 1024 * 1024
        ),
        name="owned_columns",
    )(factors, occ_energy, vir_energy.reshape(nz * group // 128, 128), start, length)


def per_device(factors, occ_energy, vir_energy, block_lengths, block_owner):
    occupied, rows, width = factors.shape
    nz, nyx = lax.axis_size("z"), lax.axis_size(ROW)
    owners = nz * nyx
    quarter = lax.axis_index(VIR)
    lengths = lax.dynamic_index_in_dim(block_lengths, quarter, 0, keepdims=False)
    owner_of = lax.dynamic_index_in_dim(block_owner, quarter, 0, keepdims=False)
    order = jnp.arange(owners, dtype=jnp.int32)
    starts = jnp.sum(jnp.where(order[None, :] < order[:, None], lengths[None, :], 0), axis=1)
    match = owner_of[None, :] == order[:, None]
    dest_start = jnp.sum(jnp.where(match, starts[None, :], 0), axis=1)
    dest_length = jnp.sum(jnp.where(match, lengths[None, :], 0), axis=1)
    got = owned_columns(factors, occ_energy, vir_energy, dest_start, dest_length)
    return jnp.transpose(got, (1, 0, 2))


def solution(mesh):
    fine = Mesh(mesh.devices.reshape(8, 4, 2, 2, 2), ("z", "y", "xl", "xh", "core"))
    placed = (P(None, ("z", "y", "xl"), VIR), P(), P(), P(), P())
    return jax.shard_map(
        per_device,
        mesh=fine,
        in_specs=placed,
        out_specs=P(("z", "y", "xl", "xh", "core"), None, None),
        check_vma=False,
    )
```
